128 devices in a mesh: section: 8 (over x_hi, y), rep: 16 (over x_lo, z, core).
Axes of the slice: x: 4 (x_hi: 2, x_lo: 2; x = x_hi * 2 + x_lo), y: 4, z: 4, core: 2. Of those that a mesh axis runs over, the one named last changes fastest.
Arguments:
- section_state: float32 [8, 4, 16, 196, 512], P('section', None, 'rep'), may hold values from -6 to 6
- arriving: float32 [2, 4, 16, 196, 512], P(None, None, 'rep'), may hold values from -6 to 6
- first_weight: float32 [8, 1, 9, 512, 128], P('section'), may hold values from -0.1875 to 0.1875
- second_weight: float32 [8, 1, 9, 512, 128], P('section'), may hold values from -0.1875 to 0.1875
Outputs:
- returned: float32 [8, 4, 16, 196, 512], P('section', None, 'rep')
- first_grad: float32 [8, 1, 9, 512, 128], P('section', None, None, 'rep')
- second_grad: float32 [8, 1, 9, 512, 128], P('section', None, None, 'rep')
The draws below stay inside these ranges and needn't reach their ends.
All inputs are finite; a program needn't handle non-finite values.
Results may differ from the reference program's by a relative error of at most 0.00019.
Values sent between devices are 32-bit elements; how exact they have to be, the bound alone decides.
A program may use at most 128 MiB of HBM per device.

```python
import jax
import jax.numpy as jnp
from jax import lax

C = 512
GROUPS = 4
SIDE = 14
BLOCKS = 1
TICKS = 3
IMAGES = 16
N_SECTION = 8


def shard_levels(key, shape, cuts, smallest, largest):
    def one(position, blocks):
        heights = jax.random.uniform(jax.random.fold_in(jax.random.fold_in(key, 6), position), (blocks,), jnp.float32, smallest / len(cuts), largest / len(cuts))
        return jnp.repeat(jnp.exp(heights), shape[position] // blocks).reshape((-1,) + (1,) * (len(shape) - position - 1))

    level = one(*cuts[0])
    for cut in cuts[1:]:
        level = level * one(*cut)
    return level


def scatter_about(rng, extent, deviation, limit, cuts=(), kind=jnp.bfloat16):
    values = deviation * jax.random.normal(rng, extent, jnp.float32)
    if cuts:
        values = values * shard_levels(rng, extent, cuts, -0.22, 0.18)
    return jnp.clip(values, -limit, limit).astype(kind)


def setup_inputs(seed: int = 0) -> dict:
    streams_of = jax.random.split(jax.random.key(seed), 5)
    section_state = scatter_about(streams_of[0], (N_SECTION, 4, IMAGES, SIDE * SIDE, C), 1.0, 6.0, ((0, 8), (2, 16)), jnp.float32)
    arriving = scatter_about(streams_of[1], (TICKS - 1, 4, IMAGES, SIDE * SIDE, C), 1.0, 6.0, ((2, 16),), jnp.float32)
    first_weight = scatter_about(streams_of[2], (N_SECTION, BLOCKS, 9, C, C // GROUPS), (9 * C // GROUPS) ** -0.5, 0.1875, ((0, 8),), jnp.float32)
    second_weight = scatter_about(streams_of[3], (N_SECTION, BLOCKS, 9, C, C // GROUPS), (9 * C // GROUPS) ** -0.5, 0.1875, ((0, 8),), jnp.float32)
    return {"section_state": section_state, "arriving": arriving, "first_weight": first_weight, "second_weight": second_weight}


def grouped_conv(inputs, weight):
    images, pixels, channels = inputs.shape
    width_group = weight.shape[2]
    groups = channels // width_group
    square = inputs.reshape(images, SIDE, SIDE, channels)
    padded = jnp.pad(square, ((0, 0), (1, 1), (1, 1), (0, 0)))
    windows = jnp.stack([padded[:, row_off:row_off + SIDE, col_off:col_off + SIDE, :].reshape(images, pixels, groups, width_group) for row_off in range(3) for col_off in range(3)])
    kernel = weight.reshape(9, groups, width_group, width_group)
    result = jnp.einsum('tgoi,tbpgi->bpgo', kernel, windows, precision=lax.Precision.HIGHEST, preferred_element_type=jnp.float32)
    return result.reshape(images, pixels, channels)

def branch_fn(inputs, weight):
    return jax.nn.silu(grouped_conv(inputs, weight))

def block_backward(halves, first_filter, second_filter):
    y_one, y_two, e_one, e_two = halves
    act_second, second_back = jax.vjp(branch_fn, y_one, second_filter)
    x_two = y_two - act_second
    act_first, first_back = jax.vjp(branch_fn, x_two, first_filter)
    x_one = y_one - act_first
    into_one, grad_second = second_back(e_two)
    total_one = e_one + into_one
    into_two, grad_first = first_back(total_one)
    return ((x_one, x_two, total_one, e_two + into_two), grad_first, grad_second)

def section_backward(halves, first_section, second_section):
    first_list = [None] * BLOCKS
    second_list = [None] * BLOCKS
    for block_index in range(BLOCKS - 1, -1, -1):
        halves, grad_first, grad_second = block_backward(halves, first_section[block_index], second_section[block_index])
        first_list[block_index] = grad_first
        second_list[block_index] = grad_second
    return (halves, jnp.stack(first_list), jnp.stack(second_list))

def reference(section_state, arriving, first_weight, second_weight):
    sections = section_state.shape[0]
    held = [tuple((section_state[section_index, member] for member in range(4))) for section_index in range(sections)]
    first_total = jnp.zeros(first_weight.shape, jnp.float32)
    second_total = jnp.zeros(second_weight.shape, jnp.float32)
    outcome = held
    for tick_index in range(TICKS):
        outcome = []
        first_parts = []
        second_parts = []
        for section_index in range(sections):
            halves, grad_first, grad_second = section_backward(held[section_index], first_weight[section_index], second_weight[section_index])
            outcome.append(halves)
            first_parts.append(grad_first)
            second_parts.append(grad_second)
        first_total = first_total + jnp.stack(first_parts)
        second_total = second_total + jnp.stack(second_parts)
        if tick_index < TICKS - 1:
            held = outcome[1:] + [tuple((arriving[tick_index, member] for member in range(4)))]
    returned = jnp.stack([jnp.stack(list(halves)) for halves in outcome])
    return (returned, first_total, second_total)
```

```python
import jax
import jax.numpy as jnp
from jax import lax
from jax.experimental import pallas as pl
from jax.experimental.pallas import tpu as pltpu
from jax.sharding import PartitionSpec as P

MESH = pl.DeviceIdType.MESH
F32, BF16 = jnp.float32, jnp.bfloat16
NT = (((1,), (1,)), ((), ()))
NN = (((1,), (0,)), ((), ()))
SIDE, PIX, PITCH, W, TAPS, GROUPS, TICKS, SECTIONS = 14, 196, 16, 128, 9, 4, 3, 8
ROWS = SIDE * PITCH
TOP = 24
FRAME = 304
HALF = 288
ORDERS = ((0, 1, 2), (1, 2, 0), (2, 0, 1))


def split(value):
    high = value.astype(BF16)
    return high, (value - high.astype(F32)).astype(BF16)


def expand(dense, frame):
    for row in range(SIDE):
        frame[pl.ds(TOP + PITCH * row, SIDE), :] = dense[pl.ds(SIDE * row, SIDE), :]


def compact(value, frame, dense):
    frame[pl.ds(TOP, ROWS), :] = value
    for row in range(SIDE):
        dense[pl.ds(SIDE * row, SIDE), :] = frame[pl.ds(TOP + PITCH * row, SIDE), :]


def shifted(frame, maps):
    for col in range(3):
        high, low = split(frame[pl.ds(TOP - PITCH - 1 + col, 256), :])
        maps[col, 0:256, :] = high
        maps[col, HALF : HALF + 256, :] = low


def tapped(maps):
    columns = []
    for tap in range(TAPS):
        row, col = divmod(tap, 3)
        first = PITCH * row
        columns.append(
            jnp.concatenate(
                [maps[col, first : first + ROWS, :], maps[col, HALF + first : HALF + first + ROWS, :]], axis=0
            )
        )
    return jnp.concatenate(columns, axis=1)


def conv(maps, weight, dims):
    out = lax.dot_general(tapped(maps), weight, dims, preferred_element_type=F32)
    return (out[:ROWS, :W] + out[:ROWS, W:]) + (out[ROWS:, :W] + out[ROWS:, W:])


def weight_grad(pulled, maps):
    high, low = split(pulled.T)
    columns = []
    for tap in range(TAPS):
        row, col = divmod(tap, 3)
        first = PITCH * row
        top = maps[col, first : first + 256, :]
        columns.append(jnp.concatenate([top, top, maps[col, HALF + first : HALF + first + 256, :]], axis=0))
    return lax.dot_general(
        jnp.concatenate([high, low, high], axis=1),
        jnp.concatenate(columns, axis=1),
        NN,
        preferred_element_type=F32,
    )


def kernel(
    state_ref, arriving_ref, first_ref, second_ref, ret_ref, fgrad_ref, sgrad_ref,
    raw, wfwd, wback, held, out, maps_y, maps_x, maps_p, der, into, e_two, frames, acc, pair, part1, part2, part3,
    wsem, lsem, ssem, rsem, osem, xsend, xrecv,
):
    section, rep = lax.axis_index("section"), lax.axis_index("rep")
    core, z, x = rep % 2, (rep // 2) % 4, rep // 8
    bit_b = z // 2
    bit_a = (z + bit_b) % 2
    bits = (x, bit_b, bit_a)

    def rep_of(x_, z_, core_):
        return x_ * 8 + z_ * 2 + core_

    across = (
        rep_of(1 - x, z, core),
        rep_of(x, 3 - z, core),
        rep_of(x, 2 * (z // 2) + 1 - z % 2, core),
    )
    mate = rep_of(x, z, 1 - core)
    below, above = (section + SECTIONS - 1) % SECTIONS, (section + 1) % SECTIONS

    barrier = pltpu.get_barrier_semaphore()
    for device in ((below, rep), (above, rep), (section, mate)) + tuple((section, r) for r in across):
        pl.semaphore_signal(barrier, inc=1, device_id=device, device_id_type=MESH)

    def lanes(g):
        return pl.ds(pl.multiple_of(g * W, W), W)

    def load_state(h, g):
        return pltpu.make_async_copy(state_ref.at[0, h, 0, :, lanes(g)], held.at[0, h, g], lsem.at[h, g])

    def load_weight(which, g):
        ref = (first_ref, second_ref)[which]
        return pltpu.make_async_copy(ref.at[0, 0, :, lanes(g), :], raw.at[which, g], wsem.at[which, g])

    def load_arriving(k, h, g):
        return pltpu.make_async_copy(
            arriving_ref.at[k, h, 0, :, lanes(g)], held.at[k + 1, h, g], rsem.at[k, h, g]
        )

    def send(k, h, g):
        return pltpu.make_async_remote_copy(
            src_ref=out.at[k, h, g],
            dst_ref=held.at[k + 1, h, g],
            send_sem=ssem.at[k, h, g],
            recv_sem=rsem.at[k, h, g],
            device_id=(below, rep),
            device_id_type=MESH,
        )

    def save(h, g):
        return pltpu.make_async_copy(out.at[2, h, g], ret_ref.at[0, h, 0, :, lanes(g)], osem.at[h, g])

    for g in range(GROUPS):
        load_state(0, g).start()
        load_weight(1, g).start()
        load_state(1, g).start()
        load_weight(0, g).start()
    for g in range(GROUPS):
        load_state(3, g).start()
        load_state(2, g).start()

    @pl.when(section == SECTIONS - 1)
    def _():
        for k in range(TICKS - 1):
            for h in range(4):
                for g in range(GROUPS):
                    load_arriving(k, h, g).start()

    frames[...] = jnp.zeros_like(frames)
    for maps in (maps_y, maps_x):
        maps[:, :, 256:HALF, :] = jnp.zeros((GROUPS, 3, HALF - 256, W), BF16)
        maps[:, :, HALF + 256 :, :] = jnp.zeros((GROUPS, 3, HALF - 256, W), BF16)
    maps_p[:, 256:HALF, :] = jnp.zeros((3, HALF - 256, W), BF16)
    maps_p[:, HALF + 256 :, :] = jnp.zeros((3, HALF - 256, W), BF16)
    inside = (lax.broadcasted_iota(jnp.int32, (ROWS, W), 0) & (PITCH - 1)) < SIDE
    frame_a, frame_b, frame_c, frame_d = (frames.at[i] for i in range(4))

    def arrive(k, h, g):
        if k == 0:
            load_state(h, g).wait()
            return

        @pl.when(section < SECTIONS - 1)
        def _():
            send(k - 1, h, g).wait_recv()

        @pl.when(section == SECTIONS - 1)
        def _():
            load_arriving(k - 1, h, g).wait()

    def leave(k, h, g):
        if k == TICKS - 1:
            save(h, g).start()
            return

        @pl.when(section > 0)
        def _():
            send(k, h, g).start()

    def prepare(which, g):
        load_weight(which, g).wait()
        for tap in range(TAPS):
            high, low = split(raw[which, g, tap])
            wfwd[which, g, 0:W, tap * W : (tap + 1) * W] = high
            wfwd[which, g, W : 2 * W, tap * W : (tap + 1) * W] = low
            back = (TAPS - 1 - tap) * W
            wback[which, g, back : back + W, 0:W] = high
            wback[which, g, back : back + W, W : 2 * W] = low

    def act_of(pre):
        gate = jax.nn.sigmoid(pre)
        return pre * gate, jnp.where(inside, gate * (1.0 + pre * (1.0 - gate)), 0.0)

    def collect(which, g, grad, fresh):
        for share in range(4):
            z_low, core_ = share // 2, share % 2
            place = acc.at[which, core_, g // 2, g % 2, (z_low + g % 2) % 2]
            rows = grad[32 * share : 32 * share + 32, :]
            place[...] = rows if fresh else place[...] + rows

    def rebuild(k, g):
        arrive(k, 0, g)
        if k == 0:
            prepare(1, g)
        expand(held.at[k, 0, g], frame_a)
        shifted(frame_a, maps_y.at[g])
        act, slope = act_of(conv(maps_y.at[g], wfwd[1, g], NT))
        der[1, g] = slope
        arrive(k, 1, g)
        expand(held.at[k, 1, g], frame_b)
        x_two = jnp.where(inside, frame_b[pl.ds(TOP, ROWS), :] - act, 0.0)
        compact(x_two, frame_c, out.at[k, 1, g])
        leave(k, 1, g)
        if k == 0:
            prepare(0, g)
        shifted(frame_c, maps_x.at[g])
        act, slope = act_of(conv(maps_x.at[g], wfwd[0, g], NT))
        der[0, g] = slope
        compact(frame_a[pl.ds(TOP, ROWS), :] - act, frame_d, out.at[k, 0, g])
        leave(k, 0, g)

    def pull_second(k, g):
        arrive(k, 3, g)
        expand(held.at[k, 3, g], frame_a)
        e_in = frame_a[pl.ds(TOP, ROWS), :]
        e_two[g] = e_in
        frame_c[pl.ds(TOP, ROWS), :] = e_in * der[1, g]
        shifted(frame_c, maps_p)
        into[g] = conv(maps_p, wback[1, g], NN)
        collect(1, g, weight_grad(frame_c[pl.ds(TOP, 256), :], maps_y.at[g]), k == 0)

    def pull_first(k, g):
        arrive(k, 2, g)
        expand(held.at[k, 2, g], frame_a)
        d_one = frame_a[pl.ds(TOP, ROWS), :] + into[g]
        compact(d_one, frame_d, out.at[k, 2, g])
        if k == TICKS - 1:
            leave(k, 2, g)
        frame_c[pl.ds(TOP, ROWS), :] = d_one * der[0, g]
        shifted(frame_c, maps_p)
        compact(e_two[g] + conv(maps_p, wback[0, g], NN), frame_d, out.at[k, 3, g])
        leave(k, 3, g)
        collect(0, g, weight_grad(frame_c[pl.ds(TOP, 256), :], maps_x.at[g]), k == 0)

    def each(function, k, first=0, last=GROUPS):
        def step(g, carry):
            function(k, g)
            return carry

        lax.fori_loop(first, last, step, 0)

    def exchange(which, level, third):
        cut = pl.ds(384 * third, 384)
        if level == 0:
            source, target, device = acc.at[which, 1 - core, :, :, :, :, cut], pair.at[which, :, :, :, :, cut], mate
        else:
            axis = ORDERS[third][level - 1]
            device = across[axis]
            if level == 1:
                index = [slice(None)] * 3
                index[axis] = 1 - bits[axis]
                source, target = pair.at[(which, *index, slice(None), cut)], part1.at[which, third]
            elif level == 2:
                rest = [a for a in range(3) if a != ORDERS[third][0]]
                index = [slice(None)] * 2
                index[rest.index(axis)] = 1 - bits[axis]
                source, target = part1.at[(which, third, *index)], part2.at[which, third]
            else:
                source, target = part2.at[which, third, 1 - bits[axis]], part3.at[which, third]
        return pltpu.make_async_remote_copy(
            src_ref=source,
            dst_ref=target,
            send_sem=xsend.at[which, level, third],
            recv_sem=xrecv.at[which, level, third],
            device_id=(section, device),
            device_id_type=MESH,
        )

    def absorb(which, level, third):
        exchange(which, level, third).wait_recv()
        cut = pl.ds(384 * third, 384)
        if level == 0:
            pair[which, :, :, :, :, cut] += acc[which, core, :, :, :, :, cut]
            return
        axis = ORDERS[third][level - 1]
        if level == 1:
            index = [slice(None)] * 3
            index[axis] = bits[axis]
            part1[which, third] += pair[(which, *index, slice(None), cut)]
        elif level == 2:
            rest = [a for a in range(3) if a != ORDERS[third][0]]
            index = [slice(None)] * 2
            index[rest.index(axis)] = bits[axis]
            part2[which, third] += part1[(which, third, *index)]
        else:
            total = part3[which, third] + part2[which, third, bits[axis]]
            grad_ref = (fgrad_ref, sgrad_ref)[which]
            for tap in range(3):
                grad_ref[0, 0, 3 * third + tap] = total[:, tap * W : (tap + 1) * W]

    def begin(which):
        for third in range(3):
            exchange(which, 0, third).start()

    def advance(which, level):
        for third in range(3):
            absorb(which, level, third)
            if level < 3:
                exchange(which, level + 1, third).start()

    pl.semaphore_wait(barrier, 6)
    for k in range(TICKS - 1):
        each(rebuild, k)
        each(pull_second, k)
        each(pull_first, k)
        each(lambda k, g: leave(k, 2, g), k)
    last = TICKS - 1
    each(rebuild, last)
    each(pull_second, last)
    begin(1)
    each(pull_first, last, 0, 2)
    advance(1, 0)
    each(pull_first, last, 2, 4)
    begin(0)
    advance(1, 1)
    advance(0, 0)
    advance(1, 2)
    advance(0, 1)
    advance(1, 3)
    advance(0, 2)
    advance(0, 3)

    def drain(g, carry):
        for h in range(4):
            save(h, g).wait()
        return carry

    lax.fori_loop(0, GROUPS, drain, 0)

    @pl.when(section > 0)
    def _():
        def drain_sent(g, carry):
            for k in range(TICKS - 1):
                for h in range(4):
                    send(k, h, g).wait_send()
            return carry

        lax.fori_loop(0, GROUPS, drain_sent, 0)

    for which in range(2):
        for level in range(4):
            for third in range(3):
                exchange(which, level, third).wait_send()


def on_device(section_state, arriving, first_weight, second_weight):
    anywhere = pl.BlockSpec(memory_space=pl.ANY)
    vmem = pl.BlockSpec(memory_space=pltpu.VMEM)
    dma = pltpu.SemaphoreType.DMA
    share = jax.ShapeDtypeStruct((1, 1, TAPS, 32, W), F32)
    return pl.pallas_call(
        kernel,
        out_shape=(jax.ShapeDtypeStruct(section_state.shape, F32), share, share),
        in_specs=[anywhere] * 4,
        out_specs=(anywhere, vmem, vmem),
        scratch_shapes=[
            pltpu.VMEM((2, GROUPS, TAPS, W, W), F32),
            pltpu.VMEM((2, GROUPS, 2 * W, TAPS * W), BF16),
            pltpu.VMEM((2, GROUPS, TAPS * W, 2 * W), BF16),
            pltpu.VMEM((TICKS, 4, GROUPS, PIX, W), F32),
            pltpu.VMEM((TICKS, 4, GROUPS, PIX, W), F32),
            pltpu.VMEM((GROUPS, 3, 2 * HALF, W), BF16),
            pltpu.VMEM((GROUPS, 3, 2 * HALF, W), BF16),
            pltpu.VMEM((3, 2 * HALF, W), BF16),
            pltpu.VMEM((2, GROUPS, ROWS, W), F32),
            pltpu.VMEM((GROUPS, ROWS, W), F32),
            pltpu.VMEM((GROUPS, ROWS, W), F32),
            pltpu.VMEM((4, FRAME, W), F32),
            pltpu.VMEM((2, 2, 2, 2, 2, 32, TAPS * W), F32),
            pltpu.VMEM((2, 2, 2, 2, 32, TAPS * W), F32),
            pltpu.VMEM((2, 3, 2, 2, 32, 384), F32),
            pltpu.VMEM((2, 3, 2, 32, 384), F32),
            pltpu.VMEM((2, 3, 32, 384), F32),
            dma((2, GROUPS)),
            dma((4, GROUPS)),
            dma((TICKS - 1, 4, GROUPS)),
            dma((TICKS - 1, 4, GROUPS)),
            dma((4, GROUPS)),
            dma((2, 4, 3)),
            dma((2, 4, 3)),
        ],
        compiler_params=pltpu.CompilerParams(
            collective_id=0, has_side_effects=True, vmem_limit_bytes=60 * 2**20
        ),
        name="relay",
    )(section_state, arriving, first_weight, second_weight)


def solution(mesh):
    return jax.shard_map(
        on_device,
        mesh=mesh,
        in_specs=(
            P("section", None, "rep", None, None),
            P(None, None, "rep", None, None),
            P("section", None, None, None, None),
            P("section", None, None, None, None),
        ),
        out_specs=(
            P("section", None, "rep", None, None),
            P("section", None, None, "rep", None),
            P("section", None, None, "rep", None),
        ),
        check_vma=False,
    )
```

```python
import jax
import jax.numpy as jnp
from jax import lax
from jax.experimental import pallas as pl
from jax.experimental.pallas import tpu as pltpu
from jax.sharding import PartitionSpec as P

MESH = pl.DeviceIdType.MESH
F32, BF16 = jnp.float32, jnp.bfloat16
NT = (((1,), (1,)), ((), ()))
NN = (((1,), (0,)), ((), ()))
SIDE, PIX, PITCH, W, TAPS, GROUPS, TICKS, SECTIONS = 14, 196, 16, 128, 9, 4, 3, 8
ROWS = SIDE * PITCH
TOP = 24
FRAME = 304
HALF = 288
ORDERS = ((0, 1, 2), (1, 2, 0), (2, 0, 1))


def split(value):
    high = value.astype(BF16)
    return high, (value - high.astype(F32)).astype(BF16)


def expand(dense, frame):
    for row in range(SIDE):
        frame[pl.ds(TOP + PITCH * row, SIDE), :] = dense[pl.ds(SIDE * row, SIDE), :]


def compact(value, frame, dense):
    frame[pl.ds(TOP, ROWS), :] = value
    for row in range(SIDE):
        dense[pl.ds(SIDE * row, SIDE), :] = frame[pl.ds(TOP + PITCH * row, SIDE), :]


def shifted(frame, maps):
    for col in range(3):
        high, low = split(frame[pl.ds(TOP - PITCH - 1 + col, 256), :])
        maps[col, 0:256, :] = high
        maps[col, HALF : HALF + 256, :] = low


def tapped(maps):
    columns = []
    for tap in range(TAPS):
        row, col = divmod(tap, 3)
        first = PITCH * row
        columns.append(
            jnp.concatenate(
                [maps[col, first : first + ROWS, :], maps[col, HALF + first : HALF + first + ROWS, :]], axis=0
            )
        )
    return jnp.concatenate(columns, axis=1)


def conv(maps, weight, dims):
    out = lax.dot_general(tapped(maps), weight, dims, preferred_element_type=F32)
    return (out[:ROWS, :W] + out[:ROWS, W:]) + (out[ROWS:, :W] + out[ROWS:, W:])


def weight_grad(pulled, maps):
    high, low = split(pulled.T)
    columns = []
    for tap in range(TAPS):
        row, col = divmod(tap, 3)
        first = PITCH * row
        top = maps[col, first : first + 256, :]
        columns.append(jnp.concatenate([top, top, maps[col, HALF + first : HALF + first + 256, :]], axis=0))
    return lax.dot_general(
        jnp.concatenate([high, low, high], axis=1),
        jnp.concatenate(columns, axis=1),
        NN,
        preferred_element_type=F32,
    )


def kernel(
    state_ref, arriving_ref, first_ref, second_ref, ret_ref, fgrad_ref, sgrad_ref,
    raw, wfwd, wback, held, out, stop, maps_y, maps_x, maps_p, der, into, e_two, frames, acc, pair, part1, part2, part3,
    wsem, lsem, ssem, rsem, osem, xsend, xrecv, psend, precv, hop_send, hop_recv,
):
    section, rep = lax.axis_index("section"), lax.axis_index("rep")
    core, z, x = rep % 2, (rep // 2) % 4, rep // 8
    bit_b = z // 2
    bit_a = (z + bit_b) % 2
    bits = (x, bit_b, bit_a)

    def rep_of(x_, z_, core_):
        return x_ * 8 + z_ * 2 + core_

    across = (
        rep_of(1 - x, z, core),
        rep_of(x, 3 - z, core),
        rep_of(x, 2 * (z // 2) + 1 - z % 2, core),
    )
    mate = rep_of(x, z, 1 - core)
    below, above = (section + SECTIONS - 1) % SECTIONS, (section + 1) % SECTIONS

    def around(steps):
        return (section // 4) * 4 + (section + steps) % 4

    came = (around(3), around(2))

    shortcut = (9 - section) % SECTIONS

    barrier = pltpu.get_barrier_semaphore()
    for device in ((below, rep), (above, rep), (around(1), rep), (around(3), rep), (shortcut, rep), (section, mate)) + tuple(
        (section, r) for r in across
    ):
        pl.semaphore_signal(barrier, inc=1, device_id=device, device_id_type=MESH)

    def lanes(g):
        return pl.ds(pl.multiple_of(g * W, W), W)

    def load_state(h, g):
        return pltpu.make_async_copy(state_ref.at[h, :, 0, lanes(g)], held.at[0, h, g], lsem.at[h, g])

    def load_weight(which, g):
        ref = (first_ref, second_ref)[which]
        return pltpu.make_async_copy(ref.at[0, 0, :, lanes(g), :], raw.at[which, g], wsem.at[which, g])

    def load_arriving(k, h, g):
        return pltpu.make_async_copy(
            arriving_ref.at[k, h, :, 0, lanes(g)], held.at[k + 1, h, g], rsem.at[k, h, g]
        )

    def send(k, h, g):
        return pltpu.make_async_remote_copy(
            src_ref=out.at[k, h, g],
            dst_ref=held.at[k + 1, h, g],
            send_sem=ssem.at[k, h, g],
            recv_sem=rsem.at[k, h, g],
            device_id=(below, rep),
            device_id_type=MESH,
        )

    def relayed(k, h, hop):
        source = (out.at[k, h, 0], stop.at[0, k, h], stop.at[1, k, h])[hop]
        target = (stop.at[0, k, h], stop.at[1, k, h], held.at[k + 1, h, 0])[hop]
        device = (around(1), around(1), (came[1] + SECTIONS - 1) % SECTIONS)[hop]
        arrived = rsem.at[k, h, 0] if hop == 2 else hop_recv.at[hop, k, h]
        return pltpu.make_async_remote_copy(
            src_ref=source,
            dst_ref=target,
            send_sem=hop_send.at[hop, k, h],
            recv_sem=arrived,
            device_id=(device, rep),
            device_id_type=MESH,
        )

    def pass_on(k, hop, halves):
        @pl.when(came[hop - 1] > 0)
        def _():
            for h in halves:
                relayed(k, h, hop - 1).wait_recv()
                relayed(k, h, hop).start()

    def save(h, g):
        return pltpu.make_async_copy(out.at[2, h, g], ret_ref.at[h, :, 0, lanes(g)], osem.at[h, g])

    for g in range(GROUPS):
        load_state(0, g).start()
        load_weight(1, g).start()
        load_state(1, g).start()
        load_weight(0, g).start()
    for g in range(GROUPS):
        load_state(3, g).start()
        load_state(2, g).start()

    @pl.when(section == SECTIONS - 1)
    def _():
        for k in range(TICKS - 1):
            for h in range(4):
                for g in range(GROUPS):
                    load_arriving(k, h, g).start()

    frames[...] = jnp.zeros_like(frames)
    for maps in (maps_y, maps_x):
        maps[:, :, 256:HALF, :] = jnp.zeros((GROUPS, 3, HALF - 256, W), BF16)
        maps[:, :, HALF + 256 :, :] = jnp.zeros((GROUPS, 3, HALF - 256, W), BF16)
    maps_p[:, 256:HALF, :] = jnp.zeros((3, HALF - 256, W), BF16)
    maps_p[:, HALF + 256 :, :] = jnp.zeros((3, HALF - 256, W), BF16)
    inside = (lax.broadcasted_iota(jnp.int32, (ROWS, W), 0) & (PITCH - 1)) < SIDE
    frame_a, frame_b, frame_c, frame_d = (frames.at[i] for i in range(4))

    def arrive(k, h, g):
        if k == 0:
            load_state(h, g).wait()
            return

        @pl.when(section < SECTIONS - 1)
        def _():
            send(k - 1, h, g).wait_recv()

        @pl.when(section == SECTIONS - 1)
        def _():
            load_arriving(k - 1, h, g).wait()

    def leave(k, h, g):
        if k == TICKS - 1:
            save(h, g).start()
            return

        @pl.when((section > 0) & (g > 0))
        def _():
            send(k, h, g).start()

        @pl.when((section > 0) & (g == 0))
        def _():
            relayed(k, h, 0).start()

    def prepare(which, g):
        load_weight(which, g).wait()
        for tap in range(TAPS):
            high, low = split(raw[which, g, tap])
            wfwd[which, g, 0:W, tap * W : (tap + 1) * W] = high
            wfwd[which, g, W : 2 * W, tap * W : (tap + 1) * W] = low
            back = (TAPS - 1 - tap) * W
            wback[which, g, back : back + W, 0:W] = high
            wback[which, g, back : back + W, W : 2 * W] = low

    def act_of(pre):
        gate = jax.nn.sigmoid(pre)
        return pre * gate, jnp.where(inside, gate * (1.0 + pre * (1.0 - gate)), 0.0)

    def collect(which, g, grad, fresh):
        for share in range(4):
            z_low, core_ = share // 2, share % 2
            place = acc.at[which, core_, g // 2, g % 2, (z_low + g % 2) % 2]
            rows = grad[32 * share : 32 * share + 32, :]
            place[...] = rows if fresh else place[...] + rows

    def rebuild(k, g):
        arrive(k, 0, g)
        if k == 0:
            prepare(1, g)
        expand(held.at[k, 0, g], frame_a)
        shifted(frame_a, maps_y.at[g])
        act, slope = act_of(conv(maps_y.at[g], wfwd[1, g], NT))
        der[1, g] = slope
        arrive(k, 1, g)
        expand(held.at[k, 1, g], frame_b)
        x_two = jnp.where(inside, frame_b[pl.ds(TOP, ROWS), :] - act, 0.0)
        compact(x_two, frame_c, out.at[k, 1, g])
        leave(k, 1, g)
        if k == 0:
            prepare(0, g)
        shifted(frame_c, maps_x.at[g])
        act, slope = act_of(conv(maps_x.at[g], wfwd[0, g], NT))
        der[0, g] = slope
        compact(frame_a[pl.ds(TOP, ROWS), :] - act, frame_d, out.at[k, 0, g])
        leave(k, 0, g)

    def pull_second(k, g):
        arrive(k, 3, g)
        expand(held.at[k, 3, g], frame_a)
        e_in = frame_a[pl.ds(TOP, ROWS), :]
        e_two[g] = e_in
        frame_c[pl.ds(TOP, ROWS), :] = e_in * der[1, g]
        shifted(frame_c, maps_p)
        into[g] = conv(maps_p, wback[1, g], NN)
        collect(1, g, weight_grad(frame_c[pl.ds(TOP, 256), :], maps_y.at[g]), k == 0)

    def pull_first(k, g):
        arrive(k, 2, g)
        expand(held.at[k, 2, g], frame_a)
        d_one = frame_a[pl.ds(TOP, ROWS), :] + into[g]
        compact(d_one, frame_d, out.at[k, 2, g])
        if k == TICKS - 1:
            leave(k, 2, g)
        else:

            @pl.when((section > 0) & (g == 0))
            def _():
                relayed(k, 2, 0).start()

        frame_c[pl.ds(TOP, ROWS), :] = d_one * der[0, g]
        shifted(frame_c, maps_p)
        compact(e_two[g] + conv(maps_p, wback[0, g], NN), frame_d, out.at[k, 3, g])
        leave(k, 3, g)
        collect(0, g, weight_grad(frame_c[pl.ds(TOP, 256), :], maps_x.at[g]), k == 0)

    def each(function, k, first=0, last=GROUPS, turn=0):
        def step(i, carry):
            function(k, (i + turn) % GROUPS if turn else i)
            return carry

        lax.fori_loop(first, last, step, 0)

    def exchange(which, level, third):
        cut = pl.ds(384 * third, 384)
        if level == 0:
            g = third
            source, target = acc.at[which, 1 - core, g // 2, g % 2], pair.at[which, g // 2, g % 2]
            return pltpu.make_async_remote_copy(
                src_ref=source,
                dst_ref=target,
                send_sem=psend.at[which, g],
                recv_sem=precv.at[which, g],
                device_id=(section, mate),
                device_id_type=MESH,
            )
        else:
            axis = ORDERS[third][level - 1]
            device = across[axis]
            if level == 1:
                index = [slice(None)] * 3
                index[axis] = 1 - bits[axis]
                source, target = pair.at[(which, *index, slice(None), cut)], part1.at[which, third]
            elif level == 2:
                rest = [a for a in range(3) if a != ORDERS[third][0]]
                index = [slice(None)] * 2
                index[rest.index(axis)] = 1 - bits[axis]
                source, target = part1.at[(which, third, *index)], part2.at[which, third]
            else:
                source, target = part2.at[which, third, 1 - bits[axis]], part3.at[which, third]
        return pltpu.make_async_remote_copy(
            src_ref=source,
            dst_ref=target,
            send_sem=xsend.at[which, level, third],
            recv_sem=xrecv.at[which, level, third],
            device_id=(section, device),
            device_id_type=MESH,
        )

    def absorb(which, level, third):
        exchange(which, level, third).wait_recv()
        cut = pl.ds(384 * third, 384)
        if level == 0:
            pair[which, third // 2, third % 2] += acc[which, core, third // 2, third % 2]
            return
        axis = ORDERS[third][level - 1]
        if level == 1:
            index = [slice(None)] * 3
            index[axis] = bits[axis]
            part1[which, third] += pair[(which, *index, slice(None), cut)]
        elif level == 2:
            rest = [a for a in range(3) if a != ORDERS[third][0]]
            index = [slice(None)] * 2
            index[rest.index(axis)] = bits[axis]
            part2[which, third] += part1[(which, third, *index)]
        else:
            total = part3[which, third] + part2[which, third, bits[axis]]
            grad_ref = (fgrad_ref, sgrad_ref)[which]
            for tap in range(3):
                grad_ref[0, 0, 3 * third + tap] = total[:, tap * W : (tap + 1) * W]

    def advance(which, level):
        for third in range(3):
            if level > 0:
                absorb(which, level, third)
            if level < 3:
                exchange(which, level + 1, third).start()

    pl.semaphore_wait(barrier, 9)
    xs, ds = (1, 0), (3, 2)

    def rebuild_1(k, g):
        rebuild(k, g)

        @pl.when(g == 1)
        def _():
            pass_on(k - 1, 2, ds)

    each(rebuild, 0)
    pass_on(0, 1, xs)
    each(pull_second, 0)
    pass_on(0, 2, xs)
    each(pull_first, 0)
    pass_on(0, 1, ds)
    each(lambda k, g: leave(k, 2, g), 0, 1)
    each(rebuild_1, 1)
    pass_on(1, 1, xs)
    each(pull_second, 1, turn=1)
    pass_on(1, 2, xs)
    each(pull_first, 1)
    pass_on(1, 1, ds)
    each(lambda k, g: leave(k, 2, g), 1, 1)
    last = TICKS - 1
    each(rebuild_1, last)

    def last_second(k, g):
        pull_second(k, g)
        exchange(1, 0, g).start()

        @pl.when(g > 0)
        def _():
            absorb(1, 0, g - 1)

    def last_first(k, g):
        pull_first(k, g)
        exchange(0, 0, g).start()

        @pl.when(g > 0)
        def _():
            absorb(0, 0, g - 1)

    each(last_second, last)
    absorb(1, 0, 3)
    advance(1, 0)
    each(last_first, last, 0, 2)
    advance(1, 1)
    each(last_first, last, 2, 4)
    absorb(0, 0, 3)
    advance(0, 0)
    advance(1, 2)
    advance(0, 1)
    advance(1, 3)
    advance(0, 2)
    advance(0, 3)

    def drain(g, carry):
        for h in range(4):
            save(h, g).wait()
        return carry

    lax.fori_loop(0, GROUPS, drain, 0)

    @pl.when(section > 0)
    def _():
        def drain_sent(g, carry):
            for k in range(TICKS - 1):
                for h in range(4):
                    send(k, h, g).wait_send()
            return carry

        lax.fori_loop(1, GROUPS, drain_sent, 0)

    for hop, condition in enumerate((section > 0, came[0] > 0, came[1] > 0)):

        @pl.when(condition)
        def _(hop=hop):
            for k in range(TICKS - 1):
                for h in range(4):
                    relayed(k, h, hop).wait_send()

    for which in range(2):
        for level in range(4):
            for third in range(3 if level else GROUPS):
                exchange(which, level, third).wait_send()


def hand_out(*refs):
    sources, results, (buffer, grads, insem, outsem) = refs[:3], refs[3:6], refs[6:]
    pieces = [(sources[0].at[h], buffer.at[h], results[0].at[h]) for h in range(4)]
    pieces += [(sources[i].at[0, 0], grads.at[i - 1], results[i].at[0, 0]) for i in (1, 2)]
    fetches = [pltpu.make_async_copy(a, b, insem.at[i]) for i, (a, b, _) in enumerate(pieces)]
    stores = [pltpu.make_async_copy(b, c, outsem.at[i]) for i, (_, b, c) in enumerate(pieces)]
    for fetch in fetches:
        fetch.start()
    for fetch, store in zip(fetches, stores):
        fetch.wait()
        store.start()
    for store in stores:
        store.wait()


def on_device(section_state, arriving, first_weight, second_weight):
    anywhere = pl.BlockSpec(memory_space=pl.ANY)
    vmem = pl.BlockSpec(memory_space=pltpu.VMEM)
    dma = pltpu.SemaphoreType.DMA
    share = jax.ShapeDtypeStruct((1, 1, TAPS, 32, W), F32)
    state = section_state.reshape(4, PIX, 1, GROUPS * W)
    coming = arriving.reshape(TICKS - 1, 4, PIX, 1, GROUPS * W)
    results = pl.pallas_call(
        kernel,
        out_shape=(jax.ShapeDtypeStruct(state.shape, F32), share, share),
        in_specs=[anywhere] * 4,
        out_specs=(anywhere, vmem, vmem),
        scratch_shapes=[
            pltpu.VMEM((2, GROUPS, TAPS, W, W), F32),
            pltpu.VMEM((2, GROUPS, 2 * W, TAPS * W), BF16),
            pltpu.VMEM((2, GROUPS, TAPS * W, 2 * W), BF16),
            pltpu.VMEM((TICKS, 4, GROUPS, PIX, W), F32),
            pltpu.VMEM((TICKS, 4, GROUPS, PIX, W), F32),
            pltpu.VMEM((2, TICKS - 1, 4, PIX, W), F32),
            pltpu.VMEM((GROUPS, 3, 2 * HALF, W), BF16),
            pltpu.VMEM((GROUPS, 3, 2 * HALF, W), BF16),
            pltpu.VMEM((3, 2 * HALF, W), BF16),
            pltpu.VMEM((2, GROUPS, ROWS, W), F32),
            pltpu.VMEM((GROUPS, ROWS, W), F32),
            pltpu.VMEM((GROUPS, ROWS, W), F32),
            pltpu.VMEM((4, FRAME, W), F32),
            pltpu.VMEM((2, 2, 2, 2, 2, 32, TAPS * W), F32),
            pltpu.VMEM((2, 2, 2, 2, 32, TAPS * W), F32),
            pltpu.VMEM((2, 3, 2, 2, 32, 384), F32),
            pltpu.VMEM((2, 3, 2, 32, 384), F32),
            pltpu.VMEM((2, 3, 32, 384), F32),
            dma((2, GROUPS)),
            dma((4, GROUPS)),
            dma((TICKS - 1, 4, GROUPS)),
            dma((TICKS - 1, 4, GROUPS)),
            dma((4, GROUPS)),
            dma((2, 4, 3)),
            dma((2, 4, 3)),
            dma((2, GROUPS)),
            dma((2, GROUPS)),
            dma((3, TICKS - 1, 4)),
            dma((2, TICKS - 1, 4)),
        ],
        compiler_params=pltpu.CompilerParams(
            collective_id=0, has_side_effects=True, vmem_limit_bytes=60 * 2**20
        ),
        name="relay",
    )(state, coming, first_weight, second_weight)
    returned, first_grad, second_grad = pl.pallas_call(
        hand_out,
        out_shape=(jax.ShapeDtypeStruct(state.shape, F32), share, share),
        in_specs=[anywhere] * 3,
        out_specs=(anywhere,) * 3,
        scratch_shapes=[pltpu.VMEM(state.shape, F32), pltpu.VMEM((2, TAPS, 32, W), F32), dma((6,)), dma((6,))],
        name="hand_out",
    )(*results)
    return returned.reshape(section_state.shape), first_grad, second_grad


def solution(mesh):
    return jax.shard_map(
        on_device,
        mesh=mesh,
        in_specs=(
            P("section", None, "rep", None, None),
            P(None, None, "rep", None, None),
            P("section", None, None, None, None),
            P("section", None, None, None, None),
        ),
        out_specs=(
            P("section", None, "rep", None, None),
            P("section", None, None, "rep", None),
            P("section", None, None, "rep", None),
        ),
        check_vma=False,
    )
```

```python
import jax
import jax.numpy as jnp
from jax import lax
from jax.experimental import pallas as pl
from jax.experimental.pallas import tpu as pltpu
from jax.sharding import PartitionSpec as P

MESH = pl.DeviceIdType.MESH
F32, BF16 = jnp.float32, jnp.bfloat16
NT = (((1,), (1,)), ((), ()))
NN = (((1,), (0,)), ((), ()))
SIDE, PIX, PITCH, W, TAPS, GROUPS, TICKS, SECTIONS = 14, 196, 16, 128, 9, 4, 3, 8
ROWS = SIDE * PITCH
TOP = 24
FRAME = 304
HALF = 288
ORDERS = ((0, 1, 2), (1, 2, 0), (2, 0, 1))

ROUND = (
    ((0, 1), (1, 0), (2, 0)),
    ((0, 2), (0, 3), (1, 3)),
)
STOPS = 3
PLAN = (
    ("R", 0, 0, (), (("h1", 0, 1, 0),)),
    ("P2", 0, 0, (("h1", 0, 0, 1),), (("h2", 0, 1, 0),)),
    ("P1", 0, 0, (("S", 0, 3, 0), ("S", 0, 3, 1), ("S", 0, 2, 1), ("h2", 0, 0, 1)), (("S", 0, 2, 0), ("h1", 0, 2, 0), ("S", 0, 3, 3), ("S", 0, 2, 3), ("S", 0, 3, 2))),
    ("R", 1, 1, (("S", 0, 2, 2), ("h1", 1, 1, 3)), ()),
    ("P2", 1, 0, (("h1", 1, 0, 2),), (("h1", 1, 0, 3), ("h2", 0, 2, 0))),
    ("P1", 1, 1, (("S", 1, 3, 3), ("S", 1, 3, 2), ("h2", 1, 0, 2), ("h2", 1, 1, 3)), (("S", 1, 3, 0), ("S", 1, 3, 1), ("h2", 1, 0, 3), ("S", 1, 2, 1))),
    ("R", 2, 0, (), (("S", 1, 2, 0), ("S", 1, 2, 2), ("S", 1, 2, 3))),
    ("P2", 2, 0, (), ()),
    ("P1", 2, 0, (("rs", 1, 0),), (("rs", 0, 0), ("rs", 1, 1), ("rs", 0, 1), ("rs", 1, 2), ("rs", 0, 2), ("rs", 1, 3), ("rs", 0, 3))),
)


def split(value):
    high = value.astype(BF16)
    return high, (value - high.astype(F32)).astype(BF16)


def expand(dense, frame):
    for row in range(SIDE):
        frame[pl.ds(TOP + PITCH * row, SIDE), :] = dense[pl.ds(SIDE * row, SIDE), :]


def compact(value, frame, dense):
    frame[pl.ds(TOP, ROWS), :] = value
    for row in range(SIDE):
        dense[pl.ds(SIDE * row, SIDE), :] = frame[pl.ds(TOP + PITCH * row, SIDE), :]


def shifted(frame, maps):
    for col in range(3):
        high, low = split(frame[pl.ds(TOP - PITCH - 1 + col, 256), :])
        maps[col, 0:256, :] = high
        maps[col, HALF : HALF + 256, :] = low


def tap_of(maps, tap):
    row, col = divmod(tap, 3)
    first = PITCH * row
    return maps[col, first : first + ROWS, :], maps[col, HALF + first : HALF + first + ROWS, :]


def conv(maps, weight):
    columns = [jnp.concatenate(tap_of(maps, tap), axis=0) for tap in range(TAPS)]
    out = lax.dot_general(jnp.concatenate(columns, axis=1), weight, NT, preferred_element_type=F32)
    return (out[:ROWS, :W] + out[:ROWS, W:]) + (out[ROWS:, :W] + out[ROWS:, W:])


def conv_back(maps, weight):
    columns = [piece for tap in range(TAPS) for piece in tap_of(maps, tap)]
    out = lax.dot_general(jnp.concatenate(columns, axis=1), weight, NN, preferred_element_type=F32)
    return out[:, :W] + out[:, W:]


def weight_grad(pulled, maps):
    high, low = split(pulled.T)
    columns = []
    for tap in range(TAPS):
        row, col = divmod(tap, 3)
        first = PITCH * row
        top = maps[col, first : first + 256, :]
        columns.append(jnp.concatenate([top, top, maps[col, HALF + first : HALF + first + 256, :]], axis=0))
    return lax.dot_general(
        jnp.concatenate([high, low, high], axis=1),
        jnp.concatenate(columns, axis=1),
        NN,
        preferred_element_type=F32,
    )


def kernel(
    state_ref, arriving_ref, first_ref, second_ref, ret_ref, fgrad_ref, sgrad_ref,
    raw, wfwd, wback, held, out, stop, maps_y, maps_x, maps_p, der, into, e_two, frames, acc, pair, part1, part2, part3,
    wsem, lsem, ssem, rsem, osem, xsend, xrecv, psend, precv, hop_send, hop_recv,
):
    section, rep = lax.axis_index("section"), lax.axis_index("rep")
    core, z, x = rep % 2, (rep // 2) % 4, rep // 8
    bit_b = z // 2
    bit_a = (z + bit_b) % 2
    bits = (x, bit_b, bit_a)

    def rep_of(x_, z_, core_):
        return x_ * 8 + z_ * 2 + core_

    across = (
        rep_of(1 - x, z, core),
        rep_of(x, 3 - z, core),
        rep_of(x, 2 * (z // 2) + 1 - z % 2, core),
    )
    mate = rep_of(x, z, 1 - core)
    below, above = (section + SECTIONS - 1) % SECTIONS, (section + 1) % SECTIONS

    def around(steps):
        return (section // 4) * 4 + (section + steps) % 4

    came = (around(3), around(2))

    shortcut = (9 - section) % SECTIONS

    barrier = pltpu.get_barrier_semaphore()
    for device in ((below, rep), (above, rep), (around(1), rep), (around(3), rep), (shortcut, rep), (section, mate)) + tuple(
        (section, r) for r in across
    ):
        pl.semaphore_signal(barrier, inc=1, device_id=device, device_id_type=MESH)

    def lanes(g):
        return pl.ds(pl.multiple_of(g * W, W), W)

    def load_state(h, g):
        return pltpu.make_async_copy(state_ref.at[h, :, 0, lanes(g)], held.at[0, h, g], lsem.at[h, g])

    def load_weight(which, g):
        ref = (first_ref, second_ref)[which]
        return pltpu.make_async_copy(ref.at[0, 0, :, lanes(g), :], raw.at[which, g], wsem.at[which, g])

    def load_arriving(k, h, g):
        return pltpu.make_async_copy(
            arriving_ref.at[k, h, :, 0, lanes(g)], held.at[k + 1, h, g], rsem.at[k, h, g]
        )

    def send(k, h, g):
        return pltpu.make_async_remote_copy(
            src_ref=out.at[k, h, g],
            dst_ref=held.at[k + 1, h, g],
            send_sem=ssem.at[k, h, g],
            recv_sem=rsem.at[k, h, g],
            device_id=(below, rep),
            device_id_type=MESH,
        )

    def relayed(k, h, g, hop):
        i = ROUND[k].index((h, g))
        source = (out.at[k, h, g], stop.at[0, k, i], stop.at[1, k, i])[hop]
        target = (stop.at[0, k, i], stop.at[1, k, i], held.at[k + 1, h, g])[hop]
        device = (around(1), around(1), (came[1] + SECTIONS - 1) % SECTIONS)[hop]
        arrived = rsem.at[k, h, g] if hop == 2 else hop_recv.at[hop, k, i]
        return pltpu.make_async_remote_copy(
            src_ref=source,
            dst_ref=target,
            send_sem=hop_send.at[hop, k, i],
            recv_sem=arrived,
            device_id=(device, rep),
            device_id_type=MESH,
        )

    def pass_on(k, h, g, hop):
        @pl.when(came[hop - 1] > 0)
        def _():
            relayed(k, h, g, hop - 1).wait_recv()
            relayed(k, h, g, hop).start()

    def save(h, g):
        return pltpu.make_async_copy(out.at[2, h, g], ret_ref.at[h, :, 0, lanes(g)], osem.at[h, g])

    for g in range(GROUPS):
        load_state(0, g).start()
        load_weight(1, g).start()
        load_state(1, g).start()
        load_weight(0, g).start()
    for g in range(GROUPS):
        load_state(3, g).start()
        load_state(2, g).start()

    @pl.when(section == SECTIONS - 1)
    def _():
        for k in range(TICKS - 1):
            for h in range(4):
                for g in range(GROUPS):
                    load_arriving(k, h, g).start()

    frames[...] = jnp.zeros_like(frames)
    for maps in (maps_y, maps_x):
        maps[:, :, 256:HALF, :] = jnp.zeros((GROUPS, 3, HALF - 256, W), BF16)
        maps[:, :, HALF + 256 :, :] = jnp.zeros((GROUPS, 3, HALF - 256, W), BF16)
    maps_p[:, :, 256:HALF, :] = jnp.zeros((2, 3, HALF - 256, W), BF16)
    maps_p[:, :, HALF + 256 :, :] = jnp.zeros((2, 3, HALF - 256, W), BF16)
    inside = (lax.broadcasted_iota(jnp.int32, (ROWS, W), 0) & (PITCH - 1)) < SIDE
    frame_a, frame_b, frame_c, frame_d = ([frames.at[i, j] for j in range(2)] for i in range(4))

    def arrive(k, h, g):
        if k == 0:
            load_state(h, g).wait()
            return

        @pl.when(section < SECTIONS - 1)
        def _():
            send(k - 1, h, g).wait_recv()

        @pl.when(section == SECTIONS - 1)
        def _():
            load_arriving(k - 1, h, g).wait()

    def leave(k, h, g):
        if k == TICKS - 1:
            save(h, g).start()
            return

        direct = section > 0
        for group in [g_ for h_, g_ in ROUND[k] if h_ == h]:
            direct = direct & (g != group)

            @pl.when((section > 0) & (g == group))
            def _(group=group):
                relayed(k, h, group, 0).start()

        @pl.when(direct)
        def _():
            send(k, h, g).start()

    def prepare(which, g):
        load_weight(which, g).wait()
        for tap in range(TAPS):
            high, low = split(raw[which, g, tap])
            wfwd[which, g, 0:W, tap * W : (tap + 1) * W] = high
            wfwd[which, g, W : 2 * W, tap * W : (tap + 1) * W] = low
            back = (TAPS - 1 - tap) * 2 * W
            wback[which, g, back : back + W, 0:W] = high
            wback[which, g, back : back + W, W : 2 * W] = low
            wback[which, g, back + W : back + 2 * W, 0:W] = high
            wback[which, g, back + W : back + 2 * W, W : 2 * W] = jnp.zeros((W, W), BF16)

    def act_of(pre):
        gate = jax.nn.sigmoid(pre)
        return pre * gate, jnp.where(inside, gate * (1.0 + pre * (1.0 - gate)), 0.0)

    def collect(which, g, grad, fresh):
        for share in range(4):
            z_low, core_ = share // 2, share % 2
            place = acc.at[which, core_, g // 2, g % 2, (z_low + g % 2) % 2]
            rows = grad[32 * share : 32 * share + 32, :]
            place[...] = rows if fresh else place[...] + rows

    def rebuild(k, pair_):
        both = [(j, 2 * pair_ + j) for j in range(2)]
        for _, g in both:
            arrive(k, 1, g)
            arrive(k, 0, g)
            if k == 0:
                prepare(1, g)
        for j, g in both:
            expand(held.at[k, 0, g], frame_a[j])
            expand(held.at[k, 1, g], frame_b[j])
        for j, g in both:
            shifted(frame_a[j], maps_y.at[g])
        acts = [act_of(conv(maps_y.at[g], wfwd[1, g])) for _, g in both]
        for (j, g), (act, slope) in zip(both, acts):
            der[1, g] = slope
            compact(jnp.where(inside, frame_b[j][pl.ds(TOP, ROWS), :] - act, 0.0), frame_c[j], out.at[k, 1, g])
        for _, g in both:
            leave(k, 1, g)
            if k == 0:
                prepare(0, g)
        for j, g in both:
            shifted(frame_c[j], maps_x.at[g])
        acts = [act_of(conv(maps_x.at[g], wfwd[0, g])) for _, g in both]
        for (j, g), (act, slope) in zip(both, acts):
            der[0, g] = slope
            compact(frame_a[j][pl.ds(TOP, ROWS), :] - act, frame_d[j], out.at[k, 0, g])
        for _, g in both:
            leave(k, 0, g)

    def pull_second(k, pair_):
        both = [(j, 2 * pair_ + j) for j in range(2)]
        for _, g in both:
            arrive(k, 3, g)
        for j, g in both:
            expand(held.at[k, 3, g], frame_a[j])
        for j, g in both:
            e_in = frame_a[j][pl.ds(TOP, ROWS), :]
            e_two[g] = e_in
            frame_c[j][pl.ds(TOP, ROWS), :] = e_in * der[1, g]
        for j, _ in both:
            shifted(frame_c[j], maps_p.at[j])
        pulled = [conv_back(maps_p.at[j], wback[1, g]) for j, g in both]
        grads = [weight_grad(frame_c[j][pl.ds(TOP, 256), :], maps_y.at[g]) for j, g in both]
        for (_, g), value, grad in zip(both, pulled, grads):
            into[g] = value
            collect(1, g, grad, k == 0)
        if k == TICKS - 1:
            for _, g in both:
                exchange(1, 0, g).start()

    def pull_first(k, pair_):
        both = [(j, 2 * pair_ + j) for j in range(2)]
        for _, g in both:
            arrive(k, 2, g)
        for j, g in both:
            expand(held.at[k, 2, g], frame_a[j])
        for j, g in both:
            d_one = frame_a[j][pl.ds(TOP, ROWS), :] + into[g]
            compact(d_one, frame_d[j], out.at[k, 2, g])
            frame_c[j][pl.ds(TOP, ROWS), :] = d_one * der[0, g]
        for j, _ in both:
            shifted(frame_c[j], maps_p.at[j])
        pulled = [conv_back(maps_p.at[j], wback[0, g]) for j, g in both]
        grads = [weight_grad(frame_c[j][pl.ds(TOP, 256), :], maps_x.at[g]) for j, g in both]
        for (j, g), value, grad in zip(both, pulled, grads):
            compact(e_two[g] + value, frame_d[j], out.at[k, 3, g])
            collect(0, g, grad, k == 0)
        if k == TICKS - 1:
            for _, g in both:
                exchange(0, 0, g).start()
            for _, g in both:
                leave(k, 2, g)
                leave(k, 3, g)

    def exchange(which, level, third):
        cut = pl.ds(384 * third, 384)
        if level == 0:
            g = third
            source, target = acc.at[which, 1 - core, g // 2, g % 2], pair.at[which, g // 2, g % 2]
            return pltpu.make_async_remote_copy(
                src_ref=source,
                dst_ref=target,
                send_sem=psend.at[which, g],
                recv_sem=precv.at[which, g],
                device_id=(section, mate),
                device_id_type=MESH,
            )
        else:
            axis = ORDERS[third][level - 1]
            device = across[axis]
            if level == 1:
                index = [slice(None)] * 3
                index[axis] = 1 - bits[axis]
                source, target = pair.at[(which, *index, slice(None), cut)], part1.at[which, third]
            elif level == 2:
                rest = [a for a in range(3) if a != ORDERS[third][0]]
                index = [slice(None)] * 2
                index[rest.index(axis)] = 1 - bits[axis]
                source, target = part1.at[(which, third, *index)], part2.at[which, third]
            else:
                source, target = part2.at[which, third, 1 - bits[axis]], part3.at[which, third]
        return pltpu.make_async_remote_copy(
            src_ref=source,
            dst_ref=target,
            send_sem=xsend.at[which, level, third],
            recv_sem=xrecv.at[which, level, third],
            device_id=(section, device),
            device_id_type=MESH,
        )

    def absorb(which, level, third):
        exchange(which, level, third).wait_recv()
        cut = pl.ds(384 * third, 384)
        if level == 0:
            pair[which, third // 2, third % 2] += acc[which, core, third // 2, third % 2]
            return
        axis = ORDERS[third][level - 1]
        if level == 1:
            index = [slice(None)] * 3
            index[axis] = bits[axis]
            part1[which, third] += pair[(which, *index, slice(None), cut)]
        elif level == 2:
            rest = [a for a in range(3) if a != ORDERS[third][0]]
            index = [slice(None)] * 2
            index[rest.index(axis)] = bits[axis]
            part2[which, third] += part1[(which, third, *index)]
        else:
            total = part3[which, third] + part2[which, third, bits[axis]]
            grad_ref = (fgrad_ref, sgrad_ref)[which]
            for tap in range(3):
                grad_ref[0, 0, 3 * third + tap] = total[:, tap * W : (tap + 1) * W]

    def advance(which, level):
        if level == 0:
            for g in range(GROUPS):
                absorb(which, 0, g)
        for third in range(3):
            if level > 0:
                absorb(which, level, third)
            if level < 3:
                exchange(which, level + 1, third).start()

    pl.semaphore_wait(barrier, 9)
    works = {"R": rebuild, "P2": pull_second, "P1": pull_first}

    def do(token):
        if token[0] == "S":
            leave(*token[1:])
        elif token[0] in ("h1", "h2"):
            pass_on(*token[1:], int(token[0][1]))
        else:
            advance(*token[1:])

    for phase, k, turn, between, after in PLAN:

        def step(i, carry, phase=phase, k=k, turn=turn, between=between):
            works[phase](k, 1 - i if turn else i)
            if between:

                @pl.when(i == 0)
                def _():
                    for token in between:
                        do(token)

            return carry

        lax.fori_loop(0, 2, step, 0)
        for token in after:
            do(token)

    def drain(g, carry):
        for h in range(4):
            save(h, g).wait()
        return carry

    lax.fori_loop(0, GROUPS, drain, 0)

    @pl.when(section > 0)
    def _():
        for k in range(TICKS - 1):
            for h in range(4):
                for g in range(GROUPS):
                    if (h, g) in ROUND[k]:
                        relayed(k, h, g, 0).wait_send()
                    else:
                        send(k, h, g).wait_send()

    for hop in (1, 2):

        @pl.when(came[hop - 1] > 0)
        def _(hop=hop):
            for k in range(TICKS - 1):
                for h, g in ROUND[k]:
                    relayed(k, h, g, hop).wait_send()

    for which in range(2):
        for level in range(4):
            for third in range(3 if level else GROUPS):
                exchange(which, level, third).wait_send()


def hand_out(*refs):
    sources, results, (buffer, grads, insem, outsem) = refs[:3], refs[3:6], refs[6:]
    pieces = [(sources[0].at[h], buffer.at[h], results[0].at[h]) for h in range(4)]
    pieces += [(sources[i].at[0, 0], grads.at[i - 1], results[i].at[0, 0]) for i in (1, 2)]
    fetches = [pltpu.make_async_copy(a, b, insem.at[i]) for i, (a, b, _) in enumerate(pieces)]
    stores = [pltpu.make_async_copy(b, c, outsem.at[i]) for i, (_, b, c) in enumerate(pieces)]
    for fetch in fetches:
        fetch.start()
    for fetch, store in zip(fetches, stores):
        fetch.wait()
        store.start()
    for store in stores:
        store.wait()


def on_device(section_state, arriving, first_weight, second_weight):
    anywhere = pl.BlockSpec(memory_space=pl.ANY)
    vmem = pl.BlockSpec(memory_space=pltpu.VMEM)
    dma = pltpu.SemaphoreType.DMA
    share = jax.ShapeDtypeStruct((1, 1, TAPS, 32, W), F32)
    state = section_state.reshape(4, PIX, 1, GROUPS * W)
    coming = arriving.reshape(TICKS - 1, 4, PIX, 1, GROUPS * W)
    results = pl.pallas_call(
        kernel,
        out_shape=(jax.ShapeDtypeStruct(state.shape, F32), share, share),
        in_specs=[anywhere] * 4,
        out_specs=(anywhere, vmem, vmem),
        scratch_shapes=[
            pltpu.VMEM((2, GROUPS, TAPS, W, W), F32),
            pltpu.VMEM((2, GROUPS, 2 * W, TAPS * W), BF16),
            pltpu.VMEM((2, GROUPS, TAPS * 2 * W, 2 * W), BF16),
            pltpu.VMEM((TICKS, 4, GROUPS, PIX, W), F32),
            pltpu.VMEM((TICKS, 4, GROUPS, PIX, W), F32),
            pltpu.VMEM((2, TICKS - 1, STOPS, PIX, W), F32),
            pltpu.VMEM((GROUPS, 3, 2 * HALF, W), BF16),
            pltpu.VMEM((GROUPS, 3, 2 * HALF, W), BF16),
            pltpu.VMEM((2, 3, 2 * HALF, W), BF16),
            pltpu.VMEM((2, GROUPS, ROWS, W), F32),
            pltpu.VMEM((GROUPS, ROWS, W), F32),
            pltpu.VMEM((GROUPS, ROWS, W), F32),
            pltpu.VMEM((4, 2, FRAME, W), F32),
            pltpu.VMEM((2, 2, 2, 2, 2, 32, TAPS * W), F32),
            pltpu.VMEM((2, 2, 2, 2, 32, TAPS * W), F32),
            pltpu.VMEM((2, 3, 2, 2, 32, 384), F32),
            pltpu.VMEM((2, 3, 2, 32, 384), F32),
            pltpu.VMEM((2, 3, 32, 384), F32),
            dma((2, GROUPS)),
            dma((4, GROUPS)),
            dma((TICKS - 1, 4, GROUPS)),
            dma((TICKS - 1, 4, GROUPS)),
            dma((4, GROUPS)),
            dma((2, 4, 3)),
            dma((2, 4, 3)),
            dma((2, GROUPS)),
            dma((2, GROUPS)),
            dma((3, TICKS - 1, STOPS)),
            dma((2, TICKS - 1, STOPS)),
        ],
        compiler_params=pltpu.CompilerParams(
            collective_id=0, has_side_effects=True, vmem_limit_bytes=60 * 2**20
        ),
        name="relay",
    )(state, coming, first_weight, second_weight)
    returned, first_grad, second_grad = pl.pallas_call(
        hand_out,
        out_shape=(jax.ShapeDtypeStruct(state.shape, F32), share, share),
        in_specs=[anywhere] * 3,
        out_specs=(anywhere,) * 3,
        scratch_shapes=[pltpu.VMEM(state.shape, F32), pltpu.VMEM((2, TAPS, 32, W), F32), dma((6,)), dma((6,))],
        name="hand_out",
    )(*results)
    return returned.reshape(section_state.shape), first_grad, second_grad


def solution(mesh):
    return jax.shard_map(
        on_device,
        mesh=mesh,
        in_specs=(
            P("section", None, "rep", None, None),
            P(None, None, "rep", None, None),
            P("section", None, None, None, None),
            P("section", None, None, None, None),
        ),
        out_specs=(
            P("section", None, "rep", None, None),
            P("section", None, None, "rep", None),
            P("section", None, None, "rep", None),
        ),
        check_vma=False,
    )
```

```python
import jax
import jax.numpy as jnp
from jax import lax
from jax.experimental import pallas as pl
from jax.experimental.pallas import tpu as pltpu
from jax.sharding import PartitionSpec as P

MESH = pl.DeviceIdType.MESH
F32, BF16 = jnp.float32, jnp.bfloat16
NT = (((1,), (1,)), ((), ()))
NN = (((1,), (0,)), ((), ()))
SIDE, PIX, PITCH, W, TAPS, GROUPS, TICKS, SECTIONS = 14, 196, 16, 128, 9, 4, 3, 8
ROWS = SIDE * PITCH
TOP = 24
FRAME = 304
HALF = 288
ORDERS = ((0, 1, 2), (1, 2, 0), (2, 0, 1))

ROUND = (
    ((1, 0), (1, 2), (2, 1)),
    ((1, 0), (1, 1), (1, 3)),
)
STOPS = 3
PLAN = (
    ("R", 0, 0, (), ()),
    ("P2", 0, 0, (("h1", 0, 1, 0),), (("h1", 0, 1, 2),)),
    ("P1", 0, 0, (), (("h2", 0, 1, 0), ("S", 0, 3, 1), ("S", 0, 3, 3), ("S", 0, 2, 2), ("h2", 0, 1, 2), ("S", 0, 2, 0), ("S", 0, 2, 3), ("S", 0, 3, 0), ("S", 0, 2, 1), ("S", 0, 3, 2))),
    ("R", 1, 1, (), (("h1", 0, 2, 1), ("h1", 1, 1, 3), ("h2", 0, 2, 1), ("h1", 1, 1, 0), ("h1", 1, 1, 1))),
    ("P2", 1, 0, (), ()),
    ("P1", 1, 0, (("S", 1, 3, 1),), (("S", 1, 3, 2), ("S", 1, 3, 0), ("h2", 1, 1, 3), ("h2", 1, 1, 0))),
    ("R", 2, 1, (("h2", 1, 1, 1), ("S", 1, 3, 3), ("S", 1, 2, 1)), (("S", 1, 2, 2), ("S", 1, 2, 3))),
    ("P2", 2, 0, (("S", 1, 2, 0),), ()),
)
LAST_TURN = 2


def split(value):
    high = value.astype(BF16)
    return high, (value - high.astype(F32)).astype(BF16)


def expand(dense, frame):
    for row in range(SIDE):
        frame[pl.ds(TOP + PITCH * row, SIDE), :] = dense[pl.ds(SIDE * row, SIDE), :]


def compact(value, frame, dense):
    frame[pl.ds(TOP, ROWS), :] = value
    for row in range(SIDE):
        dense[pl.ds(SIDE * row, SIDE), :] = frame[pl.ds(TOP + PITCH * row, SIDE), :]


def shifted(frame, maps):
    for col in range(3):
        high, low = split(frame[pl.ds(TOP - PITCH - 1 + col, 256), :])
        maps[col, 0:256, :] = high
        maps[col, HALF : HALF + 256, :] = low


def tap_of(maps, tap):
    row, col = divmod(tap, 3)
    first = PITCH * row
    return maps[col, first : first + ROWS, :], maps[col, HALF + first : HALF + first + ROWS, :]


def conv(maps, weight):
    columns = [jnp.concatenate(tap_of(maps, tap), axis=0) for tap in range(TAPS)]
    out = lax.dot_general(jnp.concatenate(columns, axis=1), weight, NT, preferred_element_type=F32)
    return (out[:ROWS, :W] + out[:ROWS, W:]) + (out[ROWS:, :W] + out[ROWS:, W:])


def conv_back(maps, weight):
    columns = [piece for tap in range(TAPS) for piece in tap_of(maps, tap)]
    out = lax.dot_general(jnp.concatenate(columns, axis=1), weight, NN, preferred_element_type=F32)
    return out[:, :W] + out[:, W:]


def weight_grad(pulled, maps):
    high, low = split(pulled.T)
    columns = []
    for tap in range(TAPS):
        row, col = divmod(tap, 3)
        first = PITCH * row
        top = maps[col, first : first + 256, :]
        columns.append(jnp.concatenate([top, top, maps[col, HALF + first : HALF + first + 256, :]], axis=0))
    return lax.dot_general(
        jnp.concatenate([high, low, high], axis=1),
        jnp.concatenate(columns, axis=1),
        NN,
        preferred_element_type=F32,
    )


def kernel(
    state_ref, arriving_ref, first_ref, second_ref, ret_ref, fgrad_ref, sgrad_ref,
    raw, wfwd, wback, held, out, stop, maps_y, maps_x, maps_p, der, into, e_two, frames, acc, pair, part1, part2, part3,
    wsem, lsem, ssem, rsem, osem, xsend, xrecv, psend, precv, lsend, lrecv, hop_send, hop_recv,
):
    section, rep = lax.axis_index("section"), lax.axis_index("rep")
    core, z, x = rep % 2, (rep // 2) % 4, rep // 8
    bit_b = z // 2
    bit_a = (z + bit_b) % 2
    bits = (x, bit_b, bit_a)

    def rep_of(x_, z_, core_):
        return x_ * 8 + z_ * 2 + core_

    across = (
        rep_of(1 - x, z, core),
        rep_of(x, 3 - z, core),
        rep_of(x, 2 * (z // 2) + 1 - z % 2, core),
    )
    mate = rep_of(x, z, 1 - core)
    below, above = (section + SECTIONS - 1) % SECTIONS, (section + 1) % SECTIONS

    def around(steps):
        return (section // 4) * 4 + (section + steps) % 4

    came = (around(3), around(2))

    shortcut = (9 - section) % SECTIONS

    barrier = pltpu.get_barrier_semaphore()
    for device in ((below, rep), (above, rep), (around(1), rep), (around(3), rep), (shortcut, rep), (section, mate)) + tuple(
        (section, r) for r in across
    ):
        pl.semaphore_signal(barrier, inc=1, device_id=device, device_id_type=MESH)

    def lanes(g):
        return pl.ds(pl.multiple_of(g * W, W), W)

    def load_state(h, g):
        return pltpu.make_async_copy(state_ref.at[h, :, 0, lanes(g)], held.at[0, h, g], lsem.at[h, g])

    def load_weight(which, g):
        ref = (first_ref, second_ref)[which]
        return pltpu.make_async_copy(ref.at[0, 0, :, lanes(g), :], raw.at[which, g], wsem.at[which, g])

    def load_arriving(k, h, g):
        return pltpu.make_async_copy(
            arriving_ref.at[k, h, :, 0, lanes(g)], held.at[k + 1, h, g], rsem.at[k, h, g]
        )

    def send(k, h, g):
        return pltpu.make_async_remote_copy(
            src_ref=out.at[k, h, g],
            dst_ref=held.at[k + 1, h, g],
            send_sem=ssem.at[k, h, g],
            recv_sem=rsem.at[k, h, g],
            device_id=(below, rep),
            device_id_type=MESH,
        )

    def relayed(k, h, g, hop):
        i = ROUND[k].index((h, g))
        source = (out.at[k, h, g], stop.at[0, k, i], stop.at[1, k, i])[hop]
        target = (stop.at[0, k, i], stop.at[1, k, i], held.at[k + 1, h, g])[hop]
        device = (around(1), around(1), (came[1] + SECTIONS - 1) % SECTIONS)[hop]
        arrived = rsem.at[k, h, g] if hop == 2 else hop_recv.at[hop, k, i]
        return pltpu.make_async_remote_copy(
            src_ref=source,
            dst_ref=target,
            send_sem=hop_send.at[hop, k, i],
            recv_sem=arrived,
            device_id=(device, rep),
            device_id_type=MESH,
        )

    def pass_on(k, h, g, hop):
        @pl.when(came[hop - 1] > 0)
        def _():
            relayed(k, h, g, hop - 1).wait_recv()
            relayed(k, h, g, hop).start()

    def save(h, g):
        return pltpu.make_async_copy(out.at[2, h, g], ret_ref.at[h, :, 0, lanes(g)], osem.at[h, g])

    for g in range(GROUPS):
        load_state(0, g).start()
        load_weight(1, g).start()
        load_state(1, g).start()
        load_weight(0, g).start()
    for g in range(GROUPS):
        load_state(3, g).start()
        load_state(2, g).start()

    @pl.when(section == SECTIONS - 1)
    def _():
        for k in range(TICKS - 1):
            for h in range(4):
                for g in range(GROUPS):
                    load_arriving(k, h, g).start()

    frames[...] = jnp.zeros_like(frames)
    for maps in (maps_y, maps_x):
        maps[:, :, 256:HALF, :] = jnp.zeros((GROUPS, 3, HALF - 256, W), BF16)
        maps[:, :, HALF + 256 :, :] = jnp.zeros((GROUPS, 3, HALF - 256, W), BF16)
    maps_p[:, :, 256:HALF, :] = jnp.zeros((2, 3, HALF - 256, W), BF16)
    maps_p[:, :, HALF + 256 :, :] = jnp.zeros((2, 3, HALF - 256, W), BF16)
    inside = (lax.broadcasted_iota(jnp.int32, (ROWS, W), 0) & (PITCH - 1)) < SIDE
    frame_a, frame_b, frame_c, frame_d = ([frames.at[i, j] for j in range(2)] for i in range(4))

    def arrive(k, h, g):
        if k == 0:
            load_state(h, g).wait()
            return

        @pl.when(section < SECTIONS - 1)
        def _():
            send(k - 1, h, g).wait_recv()

        @pl.when(section == SECTIONS - 1)
        def _():
            load_arriving(k - 1, h, g).wait()

    def leave(k, h, g):
        if k == TICKS - 1:
            save(h, g).start()
            return

        direct = section > 0
        for group in [g_ for h_, g_ in ROUND[k] if h_ == h]:
            direct = direct & (g != group)

            @pl.when((section > 0) & (g == group))
            def _(group=group):
                relayed(k, h, group, 0).start()

        @pl.when(direct)
        def _():
            send(k, h, g).start()

    def prepare(which, g):
        load_weight(which, g).wait()
        for tap in range(TAPS):
            high, low = split(raw[which, g, tap])
            wfwd[which, g, 0:W, tap * W : (tap + 1) * W] = high
            wfwd[which, g, W : 2 * W, tap * W : (tap + 1) * W] = low
            back = (TAPS - 1 - tap) * 2 * W
            wback[which, g, back : back + W, 0:W] = high
            wback[which, g, back : back + W, W : 2 * W] = low
            wback[which, g, back + W : back + 2 * W, 0:W] = high
            wback[which, g, back + W : back + 2 * W, W : 2 * W] = jnp.zeros((W, W), BF16)

    def act_of(pre):
        gate = jax.nn.sigmoid(pre)
        return pre * gate, jnp.where(inside, gate * (1.0 + pre * (1.0 - gate)), 0.0)

    def collect(which, g, grad, fresh):
        for share in range(4):
            z_low, core_ = share // 2, share % 2
            place = acc.at[which, core_, g // 2, g % 2, (z_low + g % 2) % 2]
            rows = grad[32 * share : 32 * share + 32, :]
            place[...] = rows if fresh else place[...] + rows

    def rebuild(k, pair_):
        both = [(j, 2 * pair_ + j) for j in range(2)]
        for _, g in both:
            arrive(k, 1, g)
            arrive(k, 0, g)
            if k == 0:
                prepare(1, g)
        for j, g in both:
            expand(held.at[k, 0, g], frame_a[j])
            expand(held.at[k, 1, g], frame_b[j])
        for j, g in both:
            shifted(frame_a[j], maps_y.at[g])
        acts = [act_of(conv(maps_y.at[g], wfwd[1, g])) for _, g in both]
        for (j, g), (act, slope) in zip(both, acts):
            der[1, g] = slope
            compact(jnp.where(inside, frame_b[j][pl.ds(TOP, ROWS), :] - act, 0.0), frame_c[j], out.at[k, 1, g])
        for _, g in both:
            leave(k, 1, g)
            if k == 0:
                prepare(0, g)
        for j, g in both:
            shifted(frame_c[j], maps_x.at[g])
        acts = [act_of(conv(maps_x.at[g], wfwd[0, g])) for _, g in both]
        for (j, g), (act, slope) in zip(both, acts):
            der[0, g] = slope
            compact(frame_a[j][pl.ds(TOP, ROWS), :] - act, frame_d[j], out.at[k, 0, g])
        for _, g in both:
            leave(k, 0, g)

    def pull_second(k, pair_):
        both = [(j, 2 * pair_ + j) for j in range(2)]
        for _, g in both:
            arrive(k, 3, g)
        for j, g in both:
            expand(held.at[k, 3, g], frame_a[j])
        for j, g in both:
            e_in = frame_a[j][pl.ds(TOP, ROWS), :]
            e_two[g] = e_in
            frame_c[j][pl.ds(TOP, ROWS), :] = e_in * der[1, g]
        for j, _ in both:
            shifted(frame_c[j], maps_p.at[j])
        pulled = [conv_back(maps_p.at[j], wback[1, g]) for j, g in both]
        grads = [weight_grad(frame_c[j][pl.ds(TOP, 256), :], maps_y.at[g]) for j, g in both]
        for (_, g), value, grad in zip(both, pulled, grads):
            into[g] = value
            collect(1, g, grad, k == 0)
        if k == TICKS - 1:
            for _, g in both:
                exchange(1, 0, g).start()

    def pull_first(k, pair_):
        pull_first_of(k, [(j, 2 * pair_ + j) for j in range(2)])

    def pull_first_of(k, both):
        for _, g in both:
            arrive(k, 2, g)
        for j, g in both:
            expand(held.at[k, 2, g], frame_a[j])
        for j, g in both:
            d_one = frame_a[j][pl.ds(TOP, ROWS), :] + into[g]
            compact(d_one, frame_d[j], out.at[k, 2, g])
            frame_c[j][pl.ds(TOP, ROWS), :] = d_one * der[0, g]
        for j, _ in both:
            shifted(frame_c[j], maps_p.at[j])
        pulled = [conv_back(maps_p.at[j], wback[0, g]) for j, g in both]
        grads = [weight_grad(frame_c[j][pl.ds(TOP, 256), :], maps_x.at[g]) for j, g in both]
        for (j, g), value, grad in zip(both, pulled, grads):
            compact(e_two[g] + value, frame_d[j], out.at[k, 3, g])
            collect(0, g, grad, k == 0)
        if k == TICKS - 1:
            for _, g in both:
                exchange(0, 0, g).start()
                leave(k, 2, g)
                leave(k, 3, g)

    def exchange(which, level, third):
        cut = pl.ds(384 * third, 384)
        if level == 0:
            g = third
            source, target = acc.at[which, 1 - core, g // 2, g % 2], pair.at[which, g // 2, g % 2]
            return pltpu.make_async_remote_copy(
                src_ref=source,
                dst_ref=target,
                send_sem=psend.at[which, g],
                recv_sem=precv.at[which, g],
                device_id=(section, mate),
                device_id_type=MESH,
            )
        else:
            axis = ORDERS[third][level - 1]
            device = across[axis]
            if level == 2:
                rest = [a for a in range(3) if a != ORDERS[third][0]]
                index = [slice(None)] * 2
                index[rest.index(axis)] = 1 - bits[axis]
                source, target = part1.at[(which, third, *index)], part2.at[which, third]
            else:
                source, target = part2.at[which, third, 1 - bits[axis]], part3.at[which, third]
        return pltpu.make_async_remote_copy(
            src_ref=source,
            dst_ref=target,
            send_sem=xsend.at[which, level, third],
            recv_sem=xrecv.at[which, level, third],
            device_id=(section, device),
            device_id_type=MESH,
        )

    def spread(which, third, g):
        place, cut = (g // 2, g % 2), pl.ds(384 * third, 384)
        if third == 2:
            source, target = pair.at[which, *place, 1 - bit_a, :, cut], part1.at[which, third, *place]
        else:
            source, target = pair.at[which, *place, :, :, cut], part1.at[which, third, place[1 - third]]
        return pltpu.make_async_remote_copy(
            src_ref=source,
            dst_ref=target,
            send_sem=lsend.at[which, third, g],
            recv_sem=lrecv.at[which, third, g],
            device_id=(section, across[third]),
            device_id_type=MESH,
        )

    def spreads(which, g, act, mine):
        for third in range(3):
            if third == 2:
                act(spread(which, third, g))
            else:
                side = (g // 2, g % 2)[third]

                @pl.when((bits[third] == side) if mine else (bits[third] != side))
                def _(third=third):
                    act(spread(which, third, g))

    def cascade(which, g):
        absorb(which, 0, g)
        spreads(which, g, lambda copy: copy.start(), False)

    def absorb(which, level, third):
        if level != 1:
            exchange(which, level, third).wait_recv()
        cut = pl.ds(384 * third, 384)
        if level == 0:
            pair[which, third // 2, third % 2] += acc[which, core, third // 2, third % 2]
            return
        axis = ORDERS[third][level - 1]
        if level == 1:
            index = [slice(None)] * 3
            index[axis] = bits[axis]
            part1[which, third] += pair[(which, *index, slice(None), cut)]
        elif level == 2:
            rest = [a for a in range(3) if a != ORDERS[third][0]]
            index = [slice(None)] * 2
            index[rest.index(axis)] = bits[axis]
            part2[which, third] += part1[(which, third, *index)]
        else:
            total = part3[which, third] + part2[which, third, bits[axis]]
            grad_ref = (fgrad_ref, sgrad_ref)[which]
            for tap in range(3):
                grad_ref[0, 0, 3 * third + tap] = total[:, tap * W : (tap + 1) * W]

    def advance(which, level):
        if level == 1:
            for g in range(GROUPS):
                spreads(which, g, lambda copy: copy.wait_recv(), True)
        for third in range(3):
            absorb(which, level, third)
            if level < 3:
                exchange(which, level + 1, third).start()

    pl.semaphore_wait(barrier, 9)
    works = {"R": rebuild, "P2": pull_second, "P1": pull_first}

    def do(token):
        if token[0] == "S":
            leave(*token[1:])
        else:
            pass_on(*token[1:], int(token[0][1]))

    for phase, k, turn, between, after in PLAN:

        def step(i, carry, phase=phase, k=k, turn=turn, between=between):
            works[phase](k, 1 - i if turn else i)
            if between:

                @pl.when(i == 0)
                def _():
                    for token in between:
                        do(token)

            return carry

        lax.fori_loop(0, 2, step, 0)
        for token in after:
            do(token)

    for g in range(GROUPS):
        cascade(1, g)

    def finish(i, carry):
        g = (i + LAST_TURN) % GROUPS
        pull_first_of(TICKS - 1, [(0, g)])

        @pl.when(i > 0)
        def _():
            cascade(0, (i + LAST_TURN + GROUPS - 1) % GROUPS)

        @pl.when(i == 2)
        def _():
            advance(1, 1)

        return carry

    lax.fori_loop(0, GROUPS, finish, 0)
    cascade(0, (GROUPS - 1 + LAST_TURN) % GROUPS)
    advance(1, 2)
    advance(0, 1)
    advance(1, 3)
    advance(0, 2)
    advance(0, 3)

    def drain(g, carry):
        for h in range(4):
            save(h, g).wait()
        return carry

    lax.fori_loop(0, GROUPS, drain, 0)

    @pl.when(section > 0)
    def _():
        for k in range(TICKS - 1):
            for h in range(4):
                for g in range(GROUPS):
                    if (h, g) in ROUND[k]:
                        relayed(k, h, g, 0).wait_send()
                    else:
                        send(k, h, g).wait_send()

    for hop in (1, 2):

        @pl.when(came[hop - 1] > 0)
        def _(hop=hop):
            for k in range(TICKS - 1):
                for h, g in ROUND[k]:
                    relayed(k, h, g, hop).wait_send()

    for which in range(2):
        for g in range(GROUPS):
            exchange(which, 0, g).wait_send()
            spreads(which, g, lambda copy: copy.wait_send(), False)
        for level in (2, 3):
            for third in range(3):
                exchange(which, level, third).wait_send()


def hand_out(*refs):
    sources, results, (buffer, grads, insem, outsem) = refs[:3], refs[3:6], refs[6:]
    pieces = [(sources[0].at[h], buffer.at[h], results[0].at[h]) for h in range(4)]
    pieces += [(sources[i].at[0, 0], grads.at[i - 1], results[i].at[0, 0]) for i in (1, 2)]
    fetches = [pltpu.make_async_copy(a, b, insem.at[i]) for i, (a, b, _) in enumerate(pieces)]
    stores = [pltpu.make_async_copy(b, c, outsem.at[i]) for i, (_, b, c) in enumerate(pieces)]
    for fetch in fetches:
        fetch.start()
    for fetch, store in zip(fetches, stores):
        fetch.wait()
        store.start()
    for store in stores:
        store.wait()


def on_device(section_state, arriving, first_weight, second_weight):
    anywhere = pl.BlockSpec(memory_space=pl.ANY)
    vmem = pl.BlockSpec(memory_space=pltpu.VMEM)
    dma = pltpu.SemaphoreType.DMA
    share = jax.ShapeDtypeStruct((1, 1, TAPS, 32, W), F32)
    state = section_state.reshape(4, PIX, 1, GROUPS * W)
    coming = arriving.reshape(TICKS - 1, 4, PIX, 1, GROUPS * W)
    results = pl.pallas_call(
        kernel,
        out_shape=(jax.ShapeDtypeStruct(state.shape, F32), share, share),
        in_specs=[anywhere] * 4,
        out_specs=(anywhere, vmem, vmem),
        scratch_shapes=[
            pltpu.VMEM((2, GROUPS, TAPS, W, W), F32),
            pltpu.VMEM((2, GROUPS, 2 * W, TAPS * W), BF16),
            pltpu.VMEM((2, GROUPS, TAPS * 2 * W, 2 * W), BF16),
            pltpu.VMEM((TICKS, 4, GROUPS, PIX, W), F32),
            pltpu.VMEM((TICKS, 4, GROUPS, PIX, W), F32),
            pltpu.VMEM((2, TICKS - 1, STOPS, PIX, W), F32),
            pltpu.VMEM((GROUPS, 3, 2 * HALF, W), BF16),
            pltpu.VMEM((GROUPS, 3, 2 * HALF, W), BF16),
            pltpu.VMEM((2, 3, 2 * HALF, W), BF16),
            pltpu.VMEM((2, GROUPS, ROWS, W), F32),
            pltpu.VMEM((GROUPS, ROWS, W), F32),
            pltpu.VMEM((GROUPS, ROWS, W), F32),
            pltpu.VMEM((4, 2, FRAME, W), F32),
            pltpu.VMEM((2, 2, 2, 2, 2, 32, TAPS * W), F32),
            pltpu.VMEM((2, 2, 2, 2, 32, TAPS * W), F32),
            pltpu.VMEM((2, 3, 2, 2, 32, 384), F32),
            pltpu.VMEM((2, 3, 2, 32, 384), F32),
            pltpu.VMEM((2, 3, 32, 384), F32),
            dma((2, GROUPS)),
            dma((4, GROUPS)),
            dma((TICKS - 1, 4, GROUPS)),
            dma((TICKS - 1, 4, GROUPS)),
            dma((4, GROUPS)),
            dma((2, 4, 3)),
            dma((2, 4, 3)),
            dma((2, GROUPS)),
            dma((2, GROUPS)),
            dma((2, 3, GROUPS)),
            dma((2, 3, GROUPS)),
            dma((3, TICKS - 1, STOPS)),
            dma((2, TICKS - 1, STOPS)),
        ],
        compiler_params=pltpu.CompilerParams(
            collective_id=0, has_side_effects=True, vmem_limit_bytes=60 * 2**20
        ),
        name="relay",
    )(state, coming, first_weight, second_weight)
    returned, first_grad, second_grad = pl.pallas_call(
        hand_out,
        out_shape=(jax.ShapeDtypeStruct(state.shape, F32), share, share),
        in_specs=[anywhere] * 3,
        out_specs=(anywhere,) * 3,
        scratch_shapes=[pltpu.VMEM(state.shape, F32), pltpu.VMEM((2, TAPS, 32, W), F32), dma((6,)), dma((6,))],
        name="hand_out",
    )(*results)
    return returned.reshape(section_state.shape), first_grad, second_grad


def solution(mesh):
    return jax.shard_map(
        on_device,
        mesh=mesh,
        in_specs=(
            P("section", None, "rep", None, None),
            P(None, None, "rep", None, None),
            P("section", None, None, None, None),
            P("section", None, None, None, None),
        ),
        out_specs=(
            P("section", None, "rep", None, None),
            P("section", None, None, "rep", None),
            P("section", None, None, "rep", None),
        ),
        check_vma=False,
    )
```

```python
import jax
import jax.numpy as jnp
from jax import lax
from jax.experimental import pallas as pl
from jax.experimental.pallas import tpu as pltpu
from jax.sharding import PartitionSpec as P

MESH = pl.DeviceIdType.MESH
F32, BF16 = jnp.float32, jnp.bfloat16
NT = (((1,), (1,)), ((), ()))
NN = (((1,), (0,)), ((), ()))
SIDE, PIX, PITCH, W, TAPS, GROUPS, TICKS, SECTIONS = 14, 196, 16, 128, 9, 4, 3, 8
ROWS = SIDE * PITCH
TOP = 24
FRAME = 304
HALF = 288
ORDERS = ((0, 1, 2), (1, 2, 0), (2, 0, 1))
PARTS = ((0, 2), (2, 3), (5, 4))

ROUND = (
    ((0, 0), (1, 2), (2, 0)),
    ((0, 2), (1, 2), (1, 3)),
)
STOPS = 3
PLAN = (
    ("R", 0, 1),
    ("R", 0, 0),
    ("h1", 0, 1, 2),
    ("P2", 0, 1),
    ("P1", 0, 1),
    ("h1", 0, 0, 0),
    ("P2", 0, 0),
    ("S", 0, 2, 2),
    ("S", 0, 3, 2),
    ("h2", 0, 1, 2),
    ("S", 0, 3, 3),
    ("P1", 0, 0),
    ("S", 0, 3, 0),
    ("h2", 0, 0, 0),
    ("S", 0, 3, 1),
    ("S", 0, 2, 0),
    ("S", 0, 2, 3),
    ("R", 1, 1),
    ("S", 0, 2, 1),
    ("h1", 0, 2, 0),
    ("h1", 1, 1, 3),
    ("P2", 1, 1),
    ("R", 1, 0),
    ("h2", 0, 2, 0),
    ("h1", 1, 1, 2),
    ("P2", 1, 0),
    ("P1", 1, 1),
    ("S", 1, 3, 3),
    ("h1", 1, 0, 2),
    ("P1", 1, 0),
    ("S", 1, 3, 2),
    ("h2", 1, 1, 2),
    ("S", 1, 3, 1),
    ("S", 1, 3, 0),
    ("h2", 1, 0, 2),
    ("S", 1, 2, 0),
    ("h2", 1, 1, 3),
    ("R", 2, 0),
    ("R", 2, 1),
    ("S", 1, 2, 1),
    ("S", 1, 2, 2),
    ("S", 1, 2, 3),
    ("P2", 2, 1),
    ("P2", 2, 0),
    ("P1", 2, 0),
    ("P1", 2, 1),
)


def split(value):
    high = value.astype(BF16)
    return high, (value - high.astype(F32)).astype(BF16)


def expand(dense, frame):
    for row in range(SIDE):
        frame[pl.ds(TOP + PITCH * row, SIDE), :] = dense[pl.ds(SIDE * row, SIDE), :]


def compact(value, frame, dense):
    frame[pl.ds(TOP, ROWS), :] = value
    for row in range(SIDE):
        dense[pl.ds(SIDE * row, SIDE), :] = frame[pl.ds(TOP + PITCH * row, SIDE), :]


def shifted(frame, maps):
    for col in range(3):
        high, low = split(frame[pl.ds(TOP - PITCH - 1 + col, 256), :])
        maps[col, 0:256, :] = high
        maps[col, HALF : HALF + 256, :] = low


def tap_of(maps, tap):
    row, col = divmod(tap, 3)
    first = PITCH * row
    return maps[col, first : first + ROWS, :], maps[col, HALF + first : HALF + first + ROWS, :]


def conv(maps, weight):
    columns = [jnp.concatenate(tap_of(maps, tap), axis=0) for tap in range(TAPS)]
    out = lax.dot_general(jnp.concatenate(columns, axis=1), weight, NT, preferred_element_type=F32)
    return (out[:ROWS, :W] + out[:ROWS, W:]) + (out[ROWS:, :W] + out[ROWS:, W:])


def conv_back(maps, weight):
    columns = [piece for tap in range(TAPS) for piece in tap_of(maps, tap)]
    out = lax.dot_general(jnp.concatenate(columns, axis=1), weight, NN, preferred_element_type=F32)
    return out[:, :W] + out[:, W:]


def weight_grad(pulled, maps):
    high, low = split(pulled.T)
    columns = []
    for tap in range(TAPS):
        row, col = divmod(tap, 3)
        first = PITCH * row
        top = maps[col, first : first + 256, :]
        columns.append(jnp.concatenate([top, top, maps[col, HALF + first : HALF + first + 256, :]], axis=0))
    return lax.dot_general(
        jnp.concatenate([high, low, high], axis=1),
        jnp.concatenate(columns, axis=1),
        NN,
        preferred_element_type=F32,
    )


def kernel(
    state_ref, arriving_ref, first_ref, second_ref, ret_ref, fgrad_ref, sgrad_ref,
    raw, wfwd, wback, held, out, stop, maps_y, maps_x, maps_p, der, into, e_two, frames, acc, pair, part1, part2, part3,
    wsem, lsem, ssem, rsem, osem, xsend, xrecv, psend, precv, lsend, lrecv, hop_send, hop_recv,
):
    section, rep = lax.axis_index("section"), lax.axis_index("rep")
    core, z, x = rep % 2, (rep // 2) % 4, rep // 8
    bit_b = z // 2
    bit_a = (z + bit_b) % 2
    bits = (x, bit_b, bit_a)

    def rep_of(x_, z_, core_):
        return x_ * 8 + z_ * 2 + core_

    across = (
        rep_of(1 - x, z, core),
        rep_of(x, 3 - z, core),
        rep_of(x, 2 * (z // 2) + 1 - z % 2, core),
    )
    mate = rep_of(x, z, 1 - core)
    below, above = (section + SECTIONS - 1) % SECTIONS, (section + 1) % SECTIONS

    def around(steps):
        return (section // 4) * 4 + (section + steps) % 4

    came = (around(3), around(2))

    shortcut = (9 - section) % SECTIONS

    barrier = pltpu.get_barrier_semaphore()
    for device in ((below, rep), (above, rep), (around(1), rep), (around(3), rep), (shortcut, rep), (section, mate)) + tuple(
        (section, r) for r in across
    ):
        pl.semaphore_signal(barrier, inc=1, device_id=device, device_id_type=MESH)

    def lanes(g):
        return pl.ds(pl.multiple_of(g * W, W), W)

    def load_state(h, g):
        return pltpu.make_async_copy(state_ref.at[h, :, 0, lanes(g)], held.at[0, h, g], lsem.at[h, g])

    def load_weight(which, g):
        ref = (first_ref, second_ref)[which]
        return pltpu.make_async_copy(ref.at[0, 0, :, lanes(g), :], raw.at[which, g], wsem.at[which, g])

    def load_arriving(k, h, g):
        return pltpu.make_async_copy(
            arriving_ref.at[k, h, :, 0, lanes(g)], held.at[k + 1, h, g], rsem.at[k, h, g]
        )

    def send(k, h, g):
        return pltpu.make_async_remote_copy(
            src_ref=out.at[k, h, g],
            dst_ref=held.at[k + 1, h, g],
            send_sem=ssem.at[k, h, g],
            recv_sem=rsem.at[k, h, g],
            device_id=(below, rep),
            device_id_type=MESH,
        )

    def relayed(k, h, g, hop):
        i = ROUND[k].index((h, g))
        source = (out.at[k, h, g], stop.at[0, k, i], stop.at[1, k, i])[hop]
        target = (stop.at[0, k, i], stop.at[1, k, i], held.at[k + 1, h, g])[hop]
        device = (around(1), around(1), (came[1] + SECTIONS - 1) % SECTIONS)[hop]
        arrived = rsem.at[k, h, g] if hop == 2 else hop_recv.at[hop, k, i]
        return pltpu.make_async_remote_copy(
            src_ref=source,
            dst_ref=target,
            send_sem=hop_send.at[hop, k, i],
            recv_sem=arrived,
            device_id=(device, rep),
            device_id_type=MESH,
        )

    def pass_on(k, h, g, hop):
        @pl.when(came[hop - 1] > 0)
        def _():
            relayed(k, h, g, hop - 1).wait_recv()
            relayed(k, h, g, hop).start()

    def save(h, g):
        return pltpu.make_async_copy(out.at[2, h, g], ret_ref.at[h, :, 0, lanes(g)], osem.at[h, g])

    for g in range(GROUPS):
        load_state(0, g).start()
        load_weight(1, g).start()
        load_state(1, g).start()
        load_weight(0, g).start()
    for g in range(GROUPS):
        load_state(3, g).start()
        load_state(2, g).start()

    @pl.when(section == SECTIONS - 1)
    def _():
        for k in range(TICKS - 1):
            for h in range(4):
                for g in range(GROUPS):
                    load_arriving(k, h, g).start()

    frames[...] = jnp.zeros_like(frames)
    for maps in (maps_y, maps_x):
        maps[:, :, 256:HALF, :] = jnp.zeros((GROUPS, 3, HALF - 256, W), BF16)
        maps[:, :, HALF + 256 :, :] = jnp.zeros((GROUPS, 3, HALF - 256, W), BF16)
    maps_p[:, :, 256:HALF, :] = jnp.zeros((2, 3, HALF - 256, W), BF16)
    maps_p[:, :, HALF + 256 :, :] = jnp.zeros((2, 3, HALF - 256, W), BF16)
    inside = (lax.broadcasted_iota(jnp.int32, (ROWS, W), 0) & (PITCH - 1)) < SIDE
    frame_a, frame_b, frame_c, frame_d = ([frames.at[i, j] for j in range(2)] for i in range(4))

    def arrive(k, h, g):
        if k == 0:
            load_state(h, g).wait()
            return

        @pl.when(section < SECTIONS - 1)
        def _():
            send(k - 1, h, g).wait_recv()

        @pl.when(section == SECTIONS - 1)
        def _():
            load_arriving(k - 1, h, g).wait()

    def leave(k, h, g):
        if k == TICKS - 1:
            save(h, g).start()
            return

        copy = relayed(k, h, g, 0) if (h, g) in ROUND[k] else send(k, h, g)

        @pl.when(section > 0)
        def _():
            copy.start()

    def prepare(which, g):
        load_weight(which, g).wait()
        for tap in range(TAPS):
            high, low = split(raw[which, g, tap])
            wfwd[which, g, 0:W, tap * W : (tap + 1) * W] = high
            wfwd[which, g, W : 2 * W, tap * W : (tap + 1) * W] = low
            back = (TAPS - 1 - tap) * 2 * W
            wback[which, g, back : back + W, 0:W] = high
            wback[which, g, back : back + W, W : 2 * W] = low
            wback[which, g, back + W : back + 2 * W, 0:W] = high
            wback[which, g, back + W : back + 2 * W, W : 2 * W] = jnp.zeros((W, W), BF16)

    def act_of(pre):
        gate = jax.nn.sigmoid(pre)
        return pre * gate, jnp.where(inside, gate * (1.0 + pre * (1.0 - gate)), 0.0)

    def collect(which, g, grad, fresh):
        for share in range(4):
            z_low, core_ = share // 2, share % 2
            place = acc.at[which, core_, g // 2, g % 2, (z_low + g % 2) % 2]
            rows = grad[32 * share : 32 * share + 32, :]
            place[...] = rows if fresh else place[...] + rows

    def rebuild(k, pair_):
        groups = [(j, 2 * pair_ + j) for j in range(2)]
        if (k, pair_) == PLAN[0][1:]:
            rebuild_of(k, groups[:1], True)
            rebuild_of(k, groups[1:], False)
        else:
            rebuild_of(k, groups, False)

    def rebuild_of(k, both, first):
        for _, g in both:
            arrive(k, 1, g)
            arrive(k, 0, g)
            if k == 0:
                prepare(1, g)
        for j, g in both:
            expand(held.at[k, 0, g], frame_a[j])
            expand(held.at[k, 1, g], frame_b[j])
        for j, g in both:
            shifted(frame_a[j], maps_y.at[g])
        acts = [act_of(conv(maps_y.at[g], wfwd[1, g])) for _, g in both]
        for (j, g), (act, slope) in zip(both, acts):
            der[1, g] = slope
            compact(jnp.where(inside, frame_b[j][pl.ds(TOP, ROWS), :] - act, 0.0), frame_c[j], out.at[k, 1, g])
        if first:
            pl.semaphore_wait(barrier, 9)
        for _, g in both:
            leave(k, 1, g)
        if k == 0:
            for _, g in both:
                prepare(0, g)
        for j, g in both:
            shifted(frame_c[j], maps_x.at[g])
        acts = [act_of(conv(maps_x.at[g], wfwd[0, g])) for _, g in both]
        for (j, g), (act, slope) in zip(both, acts):
            der[0, g] = slope
            compact(frame_a[j][pl.ds(TOP, ROWS), :] - act, frame_d[j], out.at[k, 0, g])
        for _, g in both:
            leave(k, 0, g)

    def pull_second(k, pair_):
        both = [(j, 2 * pair_ + j) for j in range(2)]
        for _, g in both:
            arrive(k, 3, g)
        for j, g in both:
            expand(held.at[k, 3, g], frame_a[j])
        for j, g in both:
            e_in = frame_a[j][pl.ds(TOP, ROWS), :]
            e_two[g] = e_in
            frame_c[j][pl.ds(TOP, ROWS), :] = e_in * der[1, g]
        for j, _ in both:
            shifted(frame_c[j], maps_p.at[j])
        pulled = [conv_back(maps_p.at[j], wback[1, g]) for j, g in both]
        grads = [weight_grad(frame_c[j][pl.ds(TOP, 256), :], maps_y.at[g]) for j, g in both]
        for (_, g), value, grad in zip(both, pulled, grads):
            into[g] = value
            collect(1, g, grad, k == 0)
        if k == TICKS - 1:
            for _, g in both:
                exchange(1, 0, g).start()

    def pull_first(k, pair_):
        pull_first_of(k, [(j, 2 * pair_ + j) for j in range(2)])

    def pull_first_of(k, both):
        for _, g in both:
            arrive(k, 2, g)
        for j, g in both:
            expand(held.at[k, 2, g], frame_a[j])
        for j, g in both:
            d_one = frame_a[j][pl.ds(TOP, ROWS), :] + into[g]
            compact(d_one, frame_d[j], out.at[k, 2, g])
            frame_c[j][pl.ds(TOP, ROWS), :] = d_one * der[0, g]
        for j, _ in both:
            shifted(frame_c[j], maps_p.at[j])
        last = k == TICKS - 1
        if last:
            for j, g in both:
                collect(0, g, weight_grad(frame_c[j][pl.ds(TOP, 256), :], maps_x.at[g]), False)
                exchange(0, 0, g).start()
                leave(k, 2, g)
        pulled = [conv_back(maps_p.at[j], wback[0, g]) for j, g in both]
        if not last:
            grads = [weight_grad(frame_c[j][pl.ds(TOP, 256), :], maps_x.at[g]) for j, g in both]
        for j, g in both:
            compact(e_two[g] + pulled[j], frame_d[j], out.at[k, 3, g])
            if last:
                leave(k, 3, g)
            else:
                collect(0, g, grads[j], k == 0)

    def exchange(which, level, third):
        first, count = PARTS[third % 3] if level else (0, TAPS)
        cut, width = pl.ds(W * first, W * count), pl.ds(0, W * count)
        if level == 0:
            g = third
            source, target = acc.at[which, 1 - core, g // 2, g % 2], pair.at[which, g // 2, g % 2]
            return pltpu.make_async_remote_copy(
                src_ref=source,
                dst_ref=target,
                send_sem=psend.at[which, g],
                recv_sem=precv.at[which, g],
                device_id=(section, mate),
                device_id_type=MESH,
            )
        else:
            axis = ORDERS[third][level - 1]
            device = across[axis]
            if level == 2:
                rest = [a for a in range(3) if a != ORDERS[third][0]]
                index = [slice(None)] * 2
                index[rest.index(axis)] = 1 - bits[axis]
                source = part1.at[(which, third, *index, slice(None), width)]
                target = part2.at[which, third, :, :, width]
            else:
                source = part2.at[which, third, 1 - bits[axis], :, width]
                target = part3.at[which, third, :, width]
        return pltpu.make_async_remote_copy(
            src_ref=source,
            dst_ref=target,
            send_sem=xsend.at[which, level, third],
            recv_sem=xrecv.at[which, level, third],
            device_id=(section, device),
            device_id_type=MESH,
        )

    def spread(which, third, g):
        place, (first, count) = (g // 2, g % 2), PARTS[third]
        cut, width = pl.ds(W * first, W * count), pl.ds(0, W * count)
        if third == 2:
            source = pair.at[which, *place, 1 - bit_a, :, cut]
            target = part1.at[which, third, *place, :, width]
        else:
            source = pair.at[which, *place, :, :, cut]
            target = part1.at[which, third, place[1 - third], :, :, width]
        return pltpu.make_async_remote_copy(
            src_ref=source,
            dst_ref=target,
            send_sem=lsend.at[which, third, g],
            recv_sem=lrecv.at[which, third, g],
            device_id=(section, across[third]),
            device_id_type=MESH,
        )

    def spreads(which, g, act, mine, thirds=range(3)):
        for third in thirds:
            if third == 2:
                act(spread(which, third, g))
            else:
                side = (g // 2, g % 2)[third]

                @pl.when((bits[third] == side) if mine else (bits[third] != side))
                def _(third=third):
                    act(spread(which, third, g))

    def cascade(which, g):
        absorb(which, 0, g)
        spreads(which, g, lambda copy: copy.start(), False)

    def absorb(which, level, third):
        if level == 1:
            for g in range(GROUPS):
                spreads(which, g, lambda copy: copy.wait_recv(), True, (third,))
        else:
            exchange(which, level, third).wait_recv()
        if level == 0:
            pair[which, third // 2, third % 2] += acc[which, core, third // 2, third % 2]
            return
        first, count = PARTS[third]
        cut, width = pl.ds(W * first, W * count), pl.ds(0, W * count)
        axis = ORDERS[third][level - 1]
        if level == 1:
            index = [slice(None)] * 3
            index[axis] = bits[axis]
            part1[which, third, :, :, :, width] += pair[(which, *index, slice(None), cut)]
        elif level == 2:
            rest = [a for a in range(3) if a != ORDERS[third][0]]
            index = [slice(None)] * 2
            index[rest.index(axis)] = bits[axis]
            part2[which, third, :, :, width] += part1[(which, third, *index, slice(None), width)]
        else:
            total = part3[which, third, :, width] + part2[which, third, bits[axis], :, width]
            grad_ref = (fgrad_ref, sgrad_ref)[which]
            for tap in range(count):
                grad_ref[0, 0, first + tap] = total[:, tap * W : (tap + 1) * W]

    def advance(which, level):
        for third in (2, 1, 0):
            absorb(which, level, third)
            if level < 3:
                exchange(which, level + 1, third).start()

    works = {"R": rebuild, "P2": pull_second, "P1": pull_first}

    order = [2 * token[2] + j for token in PLAN if token[:2] == ("P1", TICKS - 1) for j in range(2)]
    reduced = []
    for token in PLAN:
        kind = token[0]
        if kind == "S":
            leave(*token[1:])
            continue
        if kind in ("h1", "h2"):
            pass_on(*token[1:], int(kind[1]))
            continue
        for g in reduced:
            cascade(1, g)
        reduced = []
        k, pair_ = token[1:]
        if k < TICKS - 1 or kind != "P1":
            works[kind](k, pair_)
            if k == TICKS - 1 and kind == "P2":
                reduced = [2 * pair_, 2 * pair_ + 1]
            continue
        for g in (2 * pair_, 2 * pair_ + 1):
            i = order.index(g)
            pull_first_of(k, [(0, g)])
            if i:
                cascade(0, order[i - 1])
            if i == 2:
                advance(1, 1)
    cascade(0, order[-1])
    advance(1, 2)
    advance(0, 1)
    advance(1, 3)
    advance(0, 2)
    advance(0, 3)

    def drain(g, carry):
        for h in range(4):
            save(h, g).wait()
        return carry

    lax.fori_loop(0, GROUPS, drain, 0)

    @pl.when(section > 0)
    def _():
        for k in range(TICKS - 1):
            for h in range(4):
                for g in range(GROUPS):
                    if (h, g) in ROUND[k]:
                        relayed(k, h, g, 0).wait_send()
                    else:
                        send(k, h, g).wait_send()

    for hop in (1, 2):

        @pl.when(came[hop - 1] > 0)
        def _(hop=hop):
            for k in range(TICKS - 1):
                for h, g in ROUND[k]:
                    relayed(k, h, g, hop).wait_send()

    for which in range(2):
        for g in range(GROUPS):
            exchange(which, 0, g).wait_send()
            spreads(which, g, lambda copy: copy.wait_send(), False)
        for level in (2, 3):
            for third in range(3):
                exchange(which, level, third).wait_send()


def hand_out(*refs):
    sources, results, (buffer, grads, insem, outsem) = refs[:3], refs[3:6], refs[6:]
    pieces = [(sources[0].at[h], buffer.at[h], results[0].at[h]) for h in range(4)]
    pieces += [(sources[i].at[0, 0], grads.at[i - 1], results[i].at[0, 0]) for i in (1, 2)]
    fetches = [pltpu.make_async_copy(a, b, insem.at[i]) for i, (a, b, _) in enumerate(pieces)]
    stores = [pltpu.make_async_copy(b, c, outsem.at[i]) for i, (_, b, c) in enumerate(pieces)]
    for fetch in fetches:
        fetch.start()
    for fetch, store in zip(fetches, stores):
        fetch.wait()
        store.start()
    for store in stores:
        store.wait()


def on_device(section_state, arriving, first_weight, second_weight):
    anywhere = pl.BlockSpec(memory_space=pl.ANY)
    vmem = pl.BlockSpec(memory_space=pltpu.VMEM)
    dma = pltpu.SemaphoreType.DMA
    share = jax.ShapeDtypeStruct((1, 1, TAPS, 32, W), F32)
    state = section_state.reshape(4, PIX, 1, GROUPS * W)
    coming = arriving.reshape(TICKS - 1, 4, PIX, 1, GROUPS * W)
    results = pl.pallas_call(
        kernel,
        out_shape=(jax.ShapeDtypeStruct(state.shape, F32), share, share),
        in_specs=[anywhere] * 4,
        out_specs=(anywhere, vmem, vmem),
        scratch_shapes=[
            pltpu.VMEM((2, GROUPS, TAPS, W, W), F32),
            pltpu.VMEM((2, GROUPS, 2 * W, TAPS * W), BF16),
            pltpu.VMEM((2, GROUPS, TAPS * 2 * W, 2 * W), BF16),
            pltpu.VMEM((TICKS, 4, GROUPS, PIX, W), F32),
            pltpu.VMEM((TICKS, 4, GROUPS, PIX, W), F32),
            pltpu.VMEM((2, TICKS - 1, STOPS, PIX, W), F32),
            pltpu.VMEM((GROUPS, 3, 2 * HALF, W), BF16),
            pltpu.VMEM((GROUPS, 3, 2 * HALF, W), BF16),
            pltpu.VMEM((2, 3, 2 * HALF, W), BF16),
            pltpu.VMEM((2, GROUPS, ROWS, W), F32),
            pltpu.VMEM((GROUPS, ROWS, W), F32),
            pltpu.VMEM((GROUPS, ROWS, W), F32),
            pltpu.VMEM((4, 2, FRAME, W), F32),
            pltpu.VMEM((2, 2, 2, 2, 2, 32, TAPS * W), F32),
            pltpu.VMEM((2, 2, 2, 2, 32, TAPS * W), F32),
            pltpu.VMEM((2, 3, 2, 2, 32, 4 * W), F32),
            pltpu.VMEM((2, 3, 2, 32, 4 * W), F32),
            pltpu.VMEM((2, 3, 32, 4 * W), F32),
            dma((2, GROUPS)),
            dma((4, GROUPS)),
            dma((TICKS - 1, 4, GROUPS)),
            dma((TICKS - 1, 4, GROUPS)),
            dma((4, GROUPS)),
            dma((2, 4, 3)),
            dma((2, 4, 3)),
            dma((2, GROUPS)),
            dma((2, GROUPS)),
            dma((2, 3, GROUPS)),
            dma((2, 3, GROUPS)),
            dma((3, TICKS - 1, STOPS)),
            dma((2, TICKS - 1, STOPS)),
        ],
        compiler_params=pltpu.CompilerParams(
            collective_id=0, has_side_effects=True, vmem_limit_bytes=60 * 2**20
        ),
        name="relay",
    )(state, coming, first_weight, second_weight)
    returned, first_grad, second_grad = pl.pallas_call(
        hand_out,
        out_shape=(jax.ShapeDtypeStruct(state.shape, F32), share, share),
        in_specs=[anywhere] * 3,
        out_specs=(anywhere,) * 3,
        scratch_shapes=[pltpu.VMEM(state.shape, F32), pltpu.VMEM((2, TAPS, 32, W), F32), dma((6,)), dma((6,))],
        name="hand_out",
    )(*results)
    return returned.reshape(section_state.shape), first_grad, second_grad


def solution(mesh):
    return jax.shard_map(
        on_device,
        mesh=mesh,
        in_specs=(
            P("section", None, "rep", None, None),
            P(None, None, "rep", None, None),
            P("section", None, None, None, None),
            P("section", None, None, None, None),
        ),
        out_specs=(
            P("section", None, "rep", None, None),
            P("section", None, None, "rep", None),
            P("section", None, None, "rep", None),
        ),
        check_vma=False,
    )
```

```python
import jax
import jax.numpy as jnp
from jax import lax
from jax.experimental import pallas as pl
from jax.experimental.pallas import tpu as pltpu
from jax.sharding import PartitionSpec as P

MESH = pl.DeviceIdType.MESH
F32, BF16 = jnp.float32, jnp.bfloat16
NT = (((1,), (1,)), ((), ()))
NN = (((1,), (0,)), ((), ()))
SIDE, PIX, PITCH, W, TAPS, GROUPS, TICKS, SECTIONS = 14, 196, 16, 128, 9, 4, 3, 8
ROWS = SIDE * PITCH
TOP = 24
FRAME = 304
HALF = 288
ORDERS = ((0, 1, 2), (1, 2, 0), (2, 0, 1))
PARTS = ((0, 3), (3, 3), (6, 3))

ROUND = (
    ((0, 0), (1, 2), (2, 0)),
    ((0, 2), (1, 2), (1, 3)),
)
STOPS = 3
PLAN = (
    ("R", 0, 1),
    ("R", 0, 0),
    ("h1", 0, 1, 2),
    ("P2", 0, 1),
    ("P1", 0, 1),
    ("h1", 0, 0, 0),
    ("P2", 0, 0),
    ("S", 0, 2, 2),
    ("S", 0, 3, 2),
    ("h2", 0, 1, 2),
    ("S", 0, 3, 3),
    ("P1", 0, 0),
    ("S", 0, 3, 0),
    ("h2", 0, 0, 0),
    ("S", 0, 3, 1),
    ("S", 0, 2, 0),
    ("S", 0, 2, 3),
    ("R", 1, 1),
    ("S", 0, 2, 1),
    ("h1", 0, 2, 0),
    ("h1", 1, 1, 3),
    ("P2", 1, 1),
    ("R", 1, 0),
    ("h2", 0, 2, 0),
    ("h1", 1, 1, 2),
    ("P2", 1, 0),
    ("P1", 1, 1),
    ("S", 1, 3, 3),
    ("h1", 1, 0, 2),
    ("P1", 1, 0),
    ("S", 1, 3, 2),
    ("h2", 1, 1, 2),
    ("S", 1, 3, 1),
    ("S", 1, 3, 0),
    ("h2", 1, 0, 2),
    ("S", 1, 2, 0),
    ("h2", 1, 1, 3),
    ("R", 2, 0),
    ("R", 2, 1),
    ("S", 1, 2, 1),
    ("S", 1, 2, 2),
    ("S", 1, 2, 3),
    ("P2", 2, 1),
    ("P2", 2, 0),
    ("P1", 2, 0),
    ("P1", 2, 1),
)


def split(value):
    high = value.astype(BF16)
    return high, (value - high.astype(F32)).astype(BF16)


def expand(dense, frame):
    for row in range(SIDE):
        frame[pl.ds(TOP + PITCH * row, SIDE), :] = dense[pl.ds(SIDE * row, SIDE), :]


def compact(value, frame, dense):
    frame[pl.ds(TOP, ROWS), :] = value
    for row in range(SIDE):
        dense[pl.ds(SIDE * row, SIDE), :] = frame[pl.ds(TOP + PITCH * row, SIDE), :]


def shifted(frame, maps):
    for col in range(3):
        high, low = split(frame[pl.ds(TOP - PITCH - 1 + col, 256), :])
        maps[col, 0:256, :] = high
        maps[col, HALF : HALF + 256, :] = low


def tap_of(maps, tap):
    row, col = divmod(tap, 3)
    first = PITCH * row
    return maps[col, first : first + ROWS, :], maps[col, HALF + first : HALF + first + ROWS, :]


def conv(maps, weight):
    columns = [jnp.concatenate(tap_of(maps, tap), axis=0) for tap in range(TAPS)]
    out = lax.dot_general(jnp.concatenate(columns, axis=1), weight, NT, preferred_element_type=F32)
    return (out[:ROWS, :W] + out[:ROWS, W:]) + (out[ROWS:, :W] + out[ROWS:, W:])


def conv_back(maps, weight):
    columns = [piece for tap in range(TAPS) for piece in tap_of(maps, tap)]
    out = lax.dot_general(jnp.concatenate(columns, axis=1), weight, NN, preferred_element_type=F32)
    return out[:, :W] + out[:, W:]


def weight_grad(pulled, maps):
    high, low = split(pulled.T)
    columns = []
    for tap in range(TAPS):
        row, col = divmod(tap, 3)
        first = PITCH * row
        top = maps[col, first : first + 256, :]
        columns.append(jnp.concatenate([top, top, maps[col, HALF + first : HALF + first + 256, :]], axis=0))
    return lax.dot_general(
        jnp.concatenate([high, low, high], axis=1),
        jnp.concatenate(columns, axis=1),
        NN,
        preferred_element_type=F32,
    )


def kernel(
    state_ref, arriving_ref, first_ref, second_ref, ret_ref, fgrad_ref, sgrad_ref,
    raw, wfwd, wback, held, out, stop, maps_y, maps_x, maps_p, der, into, e_two, frames, acc, pair, part1, part2, part3,
    wsem, lsem, ssem, rsem, osem, xsend, xrecv, psend, precv, lsend, lrecv, hop_send, hop_recv,
):
    section, rep = lax.axis_index("section"), lax.axis_index("rep")
    core, z, x = rep % 2, (rep // 2) % 4, rep // 8
    bit_b = z // 2
    bit_a = (z + bit_b) % 2
    bits = (x, bit_b, bit_a)

    def rep_of(x_, z_, core_):
        return x_ * 8 + z_ * 2 + core_

    across = (
        rep_of(1 - x, z, core),
        rep_of(x, 3 - z, core),
        rep_of(x, 2 * (z // 2) + 1 - z % 2, core),
    )
    mate = rep_of(x, z, 1 - core)
    below, above = (section + SECTIONS - 1) % SECTIONS, (section + 1) % SECTIONS

    def around(steps):
        return (section // 4) * 4 + (section + steps) % 4

    came = (around(3), around(2))

    shortcut = (9 - section) % SECTIONS

    barrier = pltpu.get_barrier_semaphore()
    for device in ((below, rep), (above, rep), (around(1), rep), (around(3), rep), (shortcut, rep), (section, mate)) + tuple(
        (section, r) for r in across
    ):
        pl.semaphore_signal(barrier, inc=1, device_id=device, device_id_type=MESH)

    def lanes(g):
        return pl.ds(pl.multiple_of(g * W, W), W)

    def load_state(h, g):
        return pltpu.make_async_copy(state_ref.at[h, :, 0, lanes(g)], held.at[0, h, g], lsem.at[h, g])

    def load_weight(which, g):
        ref = (first_ref, second_ref)[which]
        return pltpu.make_async_copy(ref.at[0, 0, :, lanes(g), :], raw.at[which, g], wsem.at[which, g])

    def load_arriving(k, h, g):
        return pltpu.make_async_copy(
            arriving_ref.at[k, h, :, 0, lanes(g)], held.at[k + 1, h, g], rsem.at[k, h, g]
        )

    def send(k, h, g):
        return pltpu.make_async_remote_copy(
            src_ref=out.at[k, h, g],
            dst_ref=held.at[k + 1, h, g],
            send_sem=ssem.at[k, h, g],
            recv_sem=rsem.at[k, h, g],
            device_id=(below, rep),
            device_id_type=MESH,
        )

    def relayed(k, h, g, hop):
        i = ROUND[k].index((h, g))
        source = (out.at[k, h, g], stop.at[0, k, i], stop.at[1, k, i])[hop]
        target = (stop.at[0, k, i], stop.at[1, k, i], held.at[k + 1, h, g])[hop]
        device = (around(1), around(1), (came[1] + SECTIONS - 1) % SECTIONS)[hop]
        arrived = rsem.at[k, h, g] if hop == 2 else hop_recv.at[hop, k, i]
        return pltpu.make_async_remote_copy(
            src_ref=source,
            dst_ref=target,
            send_sem=hop_send.at[hop, k, i],
            recv_sem=arrived,
            device_id=(device, rep),
            device_id_type=MESH,
        )

    def pass_on(k, h, g, hop):
        @pl.when(came[hop - 1] > 0)
        def _():
            relayed(k, h, g, hop - 1).wait_recv()
            relayed(k, h, g, hop).start()

    def save(h, g):
        return pltpu.make_async_copy(out.at[2, h, g], ret_ref.at[h, :, 0, lanes(g)], osem.at[h, g])

    sooner = [(g + 2 * PLAN[0][2]) % GROUPS for g in range(GROUPS)]
    for g in sooner:
        load_weight(1, g).start()
        load_state(1, g).start()
        load_state(0, g).start()
        load_weight(0, g).start()
    for g in sooner:
        load_state(3, g).start()
        load_state(2, g).start()

    @pl.when(section == SECTIONS - 1)
    def _():
        for k in range(TICKS - 1):
            for h in range(4):
                for g in range(GROUPS):
                    load_arriving(k, h, g).start()

    frames[...] = jnp.zeros_like(frames)
    for maps in (maps_y, maps_x):
        maps[:, :, 256:HALF, :] = jnp.zeros((GROUPS, 3, HALF - 256, W), BF16)
        maps[:, :, HALF + 256 :, :] = jnp.zeros((GROUPS, 3, HALF - 256, W), BF16)
    maps_p[:, :, 256:HALF, :] = jnp.zeros((2, 3, HALF - 256, W), BF16)
    maps_p[:, :, HALF + 256 :, :] = jnp.zeros((2, 3, HALF - 256, W), BF16)
    inside = (lax.broadcasted_iota(jnp.int32, (ROWS, W), 0) & (PITCH - 1)) < SIDE
    frame_a, frame_b, frame_c, frame_d = ([frames.at[i, j] for j in range(2)] for i in range(4))

    def arrive(k, h, g):
        if k == 0:
            load_state(h, g).wait()
            return

        @pl.when(section < SECTIONS - 1)
        def _():
            send(k - 1, h, g).wait_recv()

        @pl.when(section == SECTIONS - 1)
        def _():
            load_arriving(k - 1, h, g).wait()

    def leave(k, h, g):
        if k == TICKS - 1:
            save(h, g).start()
            return

        copy = relayed(k, h, g, 0) if (h, g) in ROUND[k] else send(k, h, g)

        @pl.when(section > 0)
        def _():
            copy.start()

    def prepare(which, g):
        load_weight(which, g).wait()
        for tap in range(TAPS):
            high, low = split(raw[which, g, tap])
            wfwd[which, g, 0:W, tap * W : (tap + 1) * W] = high
            wfwd[which, g, W : 2 * W, tap * W : (tap + 1) * W] = low
            back = (TAPS - 1 - tap) * 2 * W
            wback[which, g, back : back + W, 0:W] = high
            wback[which, g, back : back + W, W : 2 * W] = low
            wback[which, g, back + W : back + 2 * W, 0:W] = high
            wback[which, g, back + W : back + 2 * W, W : 2 * W] = jnp.zeros((W, W), BF16)

    def act_of(pre):
        gate = jax.nn.sigmoid(pre)
        return pre * gate, jnp.where(inside, gate * (1.0 + pre * (1.0 - gate)), 0.0)

    def collect(which, g, grad, fresh):
        for share in range(4):
            z_low, core_ = share // 2, share % 2
            place = acc.at[which, core_, g // 2, g % 2, (z_low + g % 2) % 2]
            rows = grad[32 * share : 32 * share + 32, :]
            place[...] = rows if fresh else place[...] + rows

    def rebuild(k, pair_):
        groups = [(j, 2 * pair_ + j) for j in range(2)]
        if (k, pair_) == PLAN[0][1:]:
            rebuild_of(k, groups[:1], True)
            rebuild_of(k, groups[1:], False)
        else:
            rebuild_of(k, groups, False)

    def rebuild_of(k, both, first):
        for _, g in both:
            arrive(k, 1, g)
            arrive(k, 0, g)
            if k == 0:
                prepare(1, g)
        for j, g in both:
            expand(held.at[k, 0, g], frame_a[j])
            expand(held.at[k, 1, g], frame_b[j])
        for j, g in both:
            shifted(frame_a[j], maps_y.at[g])
        acts = [act_of(conv(maps_y.at[g], wfwd[1, g])) for _, g in both]
        for (j, g), (act, slope) in zip(both, acts):
            der[1, g] = slope
            compact(jnp.where(inside, frame_b[j][pl.ds(TOP, ROWS), :] - act, 0.0), frame_c[j], out.at[k, 1, g])
        if first:
            pl.semaphore_wait(barrier, 9)
        for _, g in both:
            leave(k, 1, g)
        if k == 0:
            for _, g in both:
                prepare(0, g)
        for j, g in both:
            shifted(frame_c[j], maps_x.at[g])
        acts = [act_of(conv(maps_x.at[g], wfwd[0, g])) for _, g in both]
        for (j, g), (act, slope) in zip(both, acts):
            der[0, g] = slope
            compact(frame_a[j][pl.ds(TOP, ROWS), :] - act, frame_d[j], out.at[k, 0, g])
        for _, g in both:
            leave(k, 0, g)

    def pull_second(k, pair_):
        both = [(j, 2 * pair_ + j) for j in range(2)]
        for _, g in both:
            arrive(k, 3, g)
        for j, g in both:
            expand(held.at[k, 3, g], frame_a[j])
        for j, g in both:
            e_in = frame_a[j][pl.ds(TOP, ROWS), :]
            e_two[g] = e_in
            frame_c[j][pl.ds(TOP, ROWS), :] = e_in * der[1, g]
        for j, _ in both:
            shifted(frame_c[j], maps_p.at[j])
        pulled = [conv_back(maps_p.at[j], wback[1, g]) for j, g in both]
        grads = [weight_grad(frame_c[j][pl.ds(TOP, 256), :], maps_y.at[g]) for j, g in both]
        for (_, g), value, grad in zip(both, pulled, grads):
            into[g] = value
            collect(1, g, grad, k == 0)
        if k == TICKS - 1:
            for _, g in both:
                exchange(1, 0, g).start()

    def pull_first(k, pair_):
        pull_first_of(k, [(j, 2 * pair_ + j) for j in range(2)])

    def pull_first_of(k, both):
        for _, g in both:
            arrive(k, 2, g)
        for j, g in both:
            expand(held.at[k, 2, g], frame_a[j])
        for j, g in both:
            d_one = frame_a[j][pl.ds(TOP, ROWS), :] + into[g]
            compact(d_one, frame_d[j], out.at[k, 2, g])
            frame_c[j][pl.ds(TOP, ROWS), :] = d_one * der[0, g]
        for j, _ in both:
            shifted(frame_c[j], maps_p.at[j])
        last = k == TICKS - 1
        if last:
            for j, g in both:
                collect(0, g, weight_grad(frame_c[j][pl.ds(TOP, 256), :], maps_x.at[g]), False)
                exchange(0, 0, g).start()
                leave(k, 2, g)
        pulled = [conv_back(maps_p.at[j], wback[0, g]) for j, g in both]
        if not last:
            grads = [weight_grad(frame_c[j][pl.ds(TOP, 256), :], maps_x.at[g]) for j, g in both]
        for j, g in both:
            compact(e_two[g] + pulled[j], frame_d[j], out.at[k, 3, g])
            if last:
                leave(k, 3, g)
            else:
                collect(0, g, grads[j], k == 0)

    def exchange(which, level, third):
        first, count = PARTS[third % 3] if level else (0, TAPS)
        cut, width = pl.ds(W * first, W * count), pl.ds(0, W * count)
        if level == 0:
            g = third
            source, target = acc.at[which, 1 - core, g // 2, g % 2], pair.at[which, g // 2, g % 2]
            return pltpu.make_async_remote_copy(
                src_ref=source,
                dst_ref=target,
                send_sem=psend.at[which, g],
                recv_sem=precv.at[which, g],
                device_id=(section, mate),
                device_id_type=MESH,
            )
        else:
            axis = ORDERS[third][level - 1]
            device = across[axis]
            if level == 2:
                rest = [a for a in range(3) if a != ORDERS[third][0]]
                index = [slice(None)] * 2
                index[rest.index(axis)] = 1 - bits[axis]
                source = part1.at[(which, third, *index, slice(None), width)]
                target = part2.at[which, third, :, :, width]
            else:
                source = part2.at[which, third, 1 - bits[axis], :, width]
                target = part3.at[which, third, :, width]
        return pltpu.make_async_remote_copy(
            src_ref=source,
            dst_ref=target,
            send_sem=xsend.at[which, level, third],
            recv_sem=xrecv.at[which, level, third],
            device_id=(section, device),
            device_id_type=MESH,
        )

    def spread(which, third, g):
        place, (first, count) = (g // 2, g % 2), PARTS[third]
        cut, width = pl.ds(W * first, W * count), pl.ds(0, W * count)
        if third == 2:
            source = pair.at[which, *place, 1 - bit_a, :, cut]
            target = part1.at[which, third, *place, :, width]
        else:
            source = pair.at[which, *place, :, :, cut]
            target = part1.at[which, third, place[1 - third], :, :, width]
        return pltpu.make_async_remote_copy(
            src_ref=source,
            dst_ref=target,
            send_sem=lsend.at[which, third, g],
            recv_sem=lrecv.at[which, third, g],
            device_id=(section, across[third]),
            device_id_type=MESH,
        )

    def spreads(which, g, act, mine, thirds=range(3)):
        for third in thirds:
            if third == 2:
                act(spread(which, third, g))
            else:
                side = (g // 2, g % 2)[third]

                @pl.when((bits[third] == side) if mine else (bits[third] != side))
                def _(third=third):
                    act(spread(which, third, g))

    def cascade(which, g):
        absorb(which, 0, g)
        spreads(which, g, lambda copy: copy.start(), False)

    def absorb(which, level, third):
        if level == 1:
            for g in range(GROUPS):
                spreads(which, g, lambda copy: copy.wait_recv(), True, (third,))
        else:
            exchange(which, level, third).wait_recv()
        if level == 0:
            pair[which, third // 2, third % 2] += acc[which, core, third // 2, third % 2]
            return
        first, count = PARTS[third]
        cut, width = pl.ds(W * first, W * count), pl.ds(0, W * count)
        axis = ORDERS[third][level - 1]
        if level == 1:
            index = [slice(None)] * 3
            index[axis] = bits[axis]
            part1[which, third, :, :, :, width] += pair[(which, *index, slice(None), cut)]
        elif level == 2:
            rest = [a for a in range(3) if a != ORDERS[third][0]]
            index = [slice(None)] * 2
            index[rest.index(axis)] = bits[axis]
            part2[which, third, :, :, width] += part1[(which, third, *index, slice(None), width)]
        else:
            total = part3[which, third, :, width] + part2[which, third, bits[axis], :, width]
            grad_ref = (fgrad_ref, sgrad_ref)[which]
            for tap in range(count):
                grad_ref[0, 0, first + tap] = total[:, tap * W : (tap + 1) * W]

    def advance(which, level):
        for third in (2, 1, 0):
            absorb(which, level, third)
            if level < 3:
                exchange(which, level + 1, third).start()

    works = {"R": rebuild, "P2": pull_second, "P1": pull_first}

    order = [2 * token[2] + j for token in PLAN if token[:2] == ("P1", TICKS - 1) for j in range(2)]
    reduced = []
    for token in PLAN:
        kind = token[0]
        if kind == "S":
            leave(*token[1:])
            continue
        if kind in ("h1", "h2"):
            pass_on(*token[1:], int(kind[1]))
            continue
        for g in reduced:
            cascade(1, g)
        reduced = []
        k, pair_ = token[1:]
        if k < TICKS - 1 or kind != "P1":
            works[kind](k, pair_)
            if k == TICKS - 1 and kind == "P2":
                reduced = [2 * pair_, 2 * pair_ + 1]
            continue
        for g in (2 * pair_, 2 * pair_ + 1):
            i = order.index(g)
            pull_first_of(k, [(0, g)])
            if i:
                cascade(0, order[i - 1])
            if i == 2:
                advance(1, 1)
    cascade(0, order[-1])
    advance(1, 2)
    advance(0, 1)
    advance(1, 3)
    advance(0, 2)
    advance(0, 3)

    def drain(g, carry):
        for h in range(4):
            save(h, g).wait()
        return carry

    lax.fori_loop(0, GROUPS, drain, 0)

    @pl.when(section > 0)
    def _():
        for k in range(TICKS - 1):
            for h in range(4):
                for g in range(GROUPS):
                    if (h, g) in ROUND[k]:
                        relayed(k, h, g, 0).wait_send()
                    else:
                        send(k, h, g).wait_send()

    for hop in (1, 2):

        @pl.when(came[hop - 1] > 0)
        def _(hop=hop):
            for k in range(TICKS - 1):
                for h, g in ROUND[k]:
                    relayed(k, h, g, hop).wait_send()

    for which in range(2):
        for g in range(GROUPS):
            exchange(which, 0, g).wait_send()
            spreads(which, g, lambda copy: copy.wait_send(), False)
        for level in (2, 3):
            for third in range(3):
                exchange(which, level, third).wait_send()


def hand_out(*refs):
    sources, results, (buffer, grads, insem, outsem) = refs[:3], refs[3:6], refs[6:]
    pieces = [(sources[0].at[h], buffer.at[h], results[0].at[h]) for h in range(4)]
    pieces += [(sources[i].at[0, 0], grads.at[i - 1], results[i].at[0, 0]) for i in (1, 2)]
    fetches = [pltpu.make_async_copy(a, b, insem.at[i]) for i, (a, b, _) in enumerate(pieces)]
    stores = [pltpu.make_async_copy(b, c, outsem.at[i]) for i, (_, b, c) in enumerate(pieces)]
    for fetch in fetches:
        fetch.start()
    for fetch, store in zip(fetches, stores):
        fetch.wait()
        store.start()
    for store in stores:
        store.wait()


def on_device(section_state, arriving, first_weight, second_weight):
    anywhere = pl.BlockSpec(memory_space=pl.ANY)
    vmem = pl.BlockSpec(memory_space=pltpu.VMEM)
    dma = pltpu.SemaphoreType.DMA
    share = jax.ShapeDtypeStruct((1, 1, TAPS, 32, W), F32)
    state = section_state.reshape(4, PIX, 1, GROUPS * W)
    coming = arriving.reshape(TICKS - 1, 4, PIX, 1, GROUPS * W)
    results = pl.pallas_call(
        kernel,
        out_shape=(jax.ShapeDtypeStruct(state.shape, F32), share, share),
        in_specs=[anywhere] * 4,
        out_specs=(anywhere, vmem, vmem),
        scratch_shapes=[
            pltpu.VMEM((2, GROUPS, TAPS, W, W), F32),
            pltpu.VMEM((2, GROUPS, 2 * W, TAPS * W), BF16),
            pltpu.VMEM((2, GROUPS, TAPS * 2 * W, 2 * W), BF16),
            pltpu.VMEM((TICKS, 4, GROUPS, PIX, W), F32),
            pltpu.VMEM((TICKS, 4, GROUPS, PIX, W), F32),
            pltpu.VMEM((2, TICKS - 1, STOPS, PIX, W), F32),
            pltpu.VMEM((GROUPS, 3, 2 * HALF, W), BF16),
            pltpu.VMEM((GROUPS, 3, 2 * HALF, W), BF16),
            pltpu.VMEM((2, 3, 2 * HALF, W), BF16),
            pltpu.VMEM((2, GROUPS, ROWS, W), F32),
            pltpu.VMEM((GROUPS, ROWS, W), F32),
            pltpu.VMEM((GROUPS, ROWS, W), F32),
            pltpu.VMEM((4, 2, FRAME, W), F32),
            pltpu.VMEM((2, 2, 2, 2, 2, 32, TAPS * W), F32),
            pltpu.VMEM((2, 2, 2, 2, 32, TAPS * W), F32),
            pltpu.VMEM((2, 3, 2, 2, 32, 3 * W), F32),
            pltpu.VMEM((2, 3, 2, 32, 3 * W), F32),
            pltpu.VMEM((2, 3, 32, 3 * W), F32),
            dma((2, GROUPS)),
            dma((4, GROUPS)),
            dma((TICKS - 1, 4, GROUPS)),
            dma((TICKS - 1, 4, GROUPS)),
            dma((4, GROUPS)),
            dma((2, 4, 3)),
            dma((2, 4, 3)),
            dma((2, GROUPS)),
            dma((2, GROUPS)),
            dma((2, 3, GROUPS)),
            dma((2, 3, GROUPS)),
            dma((3, TICKS - 1, STOPS)),
            dma((2, TICKS - 1, STOPS)),
        ],
        compiler_params=pltpu.CompilerParams(
            collective_id=0, has_side_effects=True, vmem_limit_bytes=60 * 2**20
        ),
        name="relay",
    )(state, coming, first_weight, second_weight)
    returned, first_grad, second_grad = pl.pallas_call(
        hand_out,
        out_shape=(jax.ShapeDtypeStruct(state.shape, F32), share, share),
        in_specs=[anywhere] * 3,
        out_specs=(anywhere,) * 3,
        scratch_shapes=[pltpu.VMEM(state.shape, F32), pltpu.VMEM((2, TAPS, 32, W), F32), dma((6,)), dma((6,))],
        name="hand_out",
    )(*results)
    return returned.reshape(section_state.shape), first_grad, second_grad


def solution(mesh):
    return jax.shard_map(
        on_device,
        mesh=mesh,
        in_specs=(
            P("section", None, "rep", None, None),
            P(None, None, "rep", None, None),
            P("section", None, None, None, None),
            P("section", None, None, None, None),
        ),
        out_specs=(
            P("section", None, "rep", None, None),
            P("section", None, None, "rep", None),
            P("section", None, None, "rep", None),
        ),
        check_vma=False,
    )
```
